512 devices in a mesh: src: 4 (over y_hi), rcv: 16 (over z, y_lo), freq: 8 (over x, core).
Axes of the slice: x: 4, y: 8 (y_hi: 4, y_lo: 2; y = y_hi * 2 + y_lo), z: 8, core: 2. Of those that a mesh axis runs over, the one named last changes fastest.
Arguments:
- wavefield: float32 [2, 8, 2048, 2048], P(None, 'freq', 'src', 'rcv'), may hold values from -6 to 6
- op_table: float32 [2, 64, 19], replicated, may hold values from -1.2 to 1.2
- vel_index: int32 [128], replicated, may hold values from 0 to 15
- interp_index: int32 [16, 8], replicated, may hold values from 0 to 62
- interp_weight: float32 [16, 8], replicated, may hold values from 0 to 1
- freq_perm: int32 [8], P('freq'), may hold values from 0 to 7, each once
Outputs:
- sunk: float32 [2, 8, 2048, 2048], P(None, 'freq', 'src', 'rcv')
- image: float32 [2048], P('rcv')
The draws below stay inside these ranges and needn't reach their ends.
Inputs may be any that keep to these rules, and one draw needn't show every extreme that they name: `freq_perm`: each of the 8 frequencies is held by exactly one slot.
All inputs are finite; a program needn't handle non-finite values.
Results may differ from the reference program's by a relative error of at most 0.00012.
Values sent between devices are 32-bit elements; how exact they have to be, the bound alone decides.
A program may use at most 64 MiB of HBM per device.

```python
import jax
import jax.numpy as jnp
from jax import lax

TAPS = 19
SUBSTEPS = 4
TILE = 16
NVEL = 16
NTAB = 64
RCV_DEV = 128
LX = 2048
NF = 8
NTILE = 128
N_RCV = 16


def place_ends(entries, stream_key, low, top_value):
    spot = [jax.random.randint(jax.random.fold_in(stream_key, axis), (), 0, length) for axis, length in enumerate(entries.shape)]
    longest = entries.shape.index(max(entries.shape))
    beside = spot[:longest] + [(spot[longest] + 1) % entries.shape[longest]] + spot[longest + 1:]
    return entries.at[tuple(spot)].set(low).at[tuple(beside)].set(top_value)


def steps_of(key, shape, split, least, high):
    def one(position, blocks):
        steps = jax.random.uniform(jax.random.fold_in(jax.random.fold_in(key, 6), position), (blocks,), jnp.float32, least / len(split), high / len(split))
        return jnp.repeat(jnp.exp(steps), shape[position] // blocks).reshape((-1,) + (1,) * (len(shape) - position - 1))

    level = one(*split[0])
    for cut in split[1:]:
        level = level * one(*cut)
    return level


def bell_draw(key, extent, scale, reach, split=(), kind=jnp.bfloat16):
    level = steps_of(key, extent, split, -0.22, 0.18) if split else 1.0
    entries = jax.random.normal(key, extent, jnp.float32) * scale * level
    return jnp.minimum(jnp.maximum(entries, -reach), reach).astype(kind)


def setup_inputs(seed: int = 0) -> dict:
    streams_of = jax.random.split(jax.random.key(seed), 7)
    wavefield = bell_draw(streams_of[0], (2, NF, LX, LX), 1.0, 6.0, ((1, 8), (2, 4), (3, 16)), jnp.float32)
    op_table = bell_draw(streams_of[1], (2, NTAB, TAPS), 0.2, 1.2, (), jnp.float32)
    vel_index = place_ends(jax.random.randint(streams_of[2], (NTILE,), 0, NVEL), jax.random.fold_in(streams_of[2], 1), 0, NVEL - 1).astype(jnp.int32)
    interp_index = place_ends(jax.random.randint(streams_of[3], (NVEL, NF), 0, NTAB - 1), jax.random.fold_in(streams_of[3], 1), 0, (NTAB - 1) - 1).astype(jnp.int32)
    interp_weight = jnp.clip(jax.random.uniform(streams_of[4], (NVEL, NF), jnp.float32, 0.0, 1.0), 0.0, 1.0)
    freq_perm = jax.random.permutation(streams_of[5], NF).astype(jnp.int32)
    return dict(wavefield=wavefield, op_table=op_table, vel_index=vel_index, interp_index=interp_index, interp_weight=interp_weight, freq_perm=freq_perm)


def convolve(padded, coef_slot, along_axis, span_width):
    real_acc = None
    imag_acc = None
    for tap_index in range(coef_slot.shape[1]):
        window = lax.slice_in_dim(padded, tap_index, tap_index + span_width, axis=along_axis)
        coef_real = coef_slot[0, tap_index]
        coef_imag = coef_slot[1, tap_index]
        if along_axis == 2:
            coef_real = coef_real[None, :]
            coef_imag = coef_imag[None, :]
        else:
            coef_real = coef_real[:, None]
            coef_imag = coef_imag[:, None]
        term_real = coef_real * window[0] - coef_imag * window[1]
        term_imag = coef_real * window[1] + coef_imag * window[0]
        if real_acc is None:
            real_acc, imag_acc = term_real, term_imag
        else:
            real_acc = real_acc + term_real
            imag_acc = imag_acc + term_imag
    return jnp.stack([real_acc, imag_acc])


def reference(wavefield, op_table, vel_index, interp_index, interp_weight, freq_perm):
    table_row = interp_index[:, freq_perm]
    weights = interp_weight[:, freq_perm]
    lower_taps = op_table[:, table_row]
    upper_taps = op_table[:, table_row + 1]
    mixed = lower_taps * (1.0 - weights)[None, :, :, None] + upper_taps * weights[None, :, :, None]
    mixed_taps = jnp.transpose(mixed, (0, 2, 3, 1))
    velocity = vel_index[jnp.arange(LX) // TILE]
    coefficients = mixed_taps[..., velocity]
    half_taps = TAPS // 2

    def one_frequency(slot, carry):
        sunk_all, image_acc = carry
        field = lax.dynamic_index_in_dim(wavefield, slot, axis=1, keepdims=False)
        coef_slot = lax.dynamic_index_in_dim(coefficients, slot, axis=1, keepdims=False)

        def receiver_block(block, current):
            piece = lax.dynamic_slice_in_dim(current, block * RCV_DEV, RCV_DEV, axis=1)
            for substep in range(SUBSTEPS):
                padded = jnp.pad(piece, ((0, 0), (0, 0), (half_taps, half_taps)))
                piece = convolve(padded, coef_slot, 2, LX)
            return lax.dynamic_update_slice_in_dim(current, piece, block * RCV_DEV, axis=1)

        def source_block(block, current):
            piece = lax.dynamic_slice_in_dim(current, block * RCV_DEV, RCV_DEV, axis=2)
            for substep in range(SUBSTEPS):
                padded = jnp.pad(piece, ((0, 0), (half_taps, half_taps), (0, 0)))
                piece = convolve(padded, coef_slot, 1, LX)
            return lax.dynamic_update_slice_in_dim(current, piece, block * RCV_DEV, axis=2)

        field = lax.fori_loop(0, N_RCV, receiver_block, field)
        field = lax.fori_loop(0, N_RCV, source_block, field)
        sunk_all = lax.dynamic_update_index_in_dim(sunk_all, field, slot, axis=1)
        image_acc = image_acc + jnp.diagonal(field[0])
        return (sunk_all, image_acc)

    start_sunk = jnp.zeros_like(wavefield)
    start_image = jnp.zeros((LX,), wavefield.dtype)
    sunk, image = lax.fori_loop(0, NF, one_frequency, (start_sunk, start_image))
    return sunk, image
```

```python
import functools

import jax
import jax.numpy as jnp
from jax import lax
from jax.experimental import pallas as pl
from jax.experimental.pallas import tpu as pltpu
from jax.sharding import PartitionSpec as P

MESH = pl.DeviceIdType.MESH
F32 = jnp.float32
BF = jnp.bfloat16
TILE = 16
TAPS = 19
HALO = 36
BLK = 128
PAD = 64
WIN = 256
SLAB = 72


def split(x):
    hi = x.astype(BF)
    return hi, (x - hi.astype(F32)).astype(BF)


def dot3(ah, al, bh, bl):
    a = jnp.concatenate([ah, al, ah], axis=1)
    b = jnp.concatenate([bh, bh, bl], axis=0)
    return jnp.dot(a, b, preferred_element_type=F32)


def rows(a, b):
    return jnp.concatenate([a, b], axis=0)


def lanes(a, b):
    return jnp.concatenate([a, b], axis=1)


def operator_block(cr, ci):
    ar = pltpu.roll(cr, 0, 1, stride=1, stride_axis=0)
    ai = pltpu.roll(ci, 0, 1, stride=1, stride_axis=0)
    rh, rl = split(ar)
    ih, il = split(ai)
    o = dot3(rows(rh, ih), rows(rl, il), lanes(rh, ih), lanes(rl, il))
    br = o[:WIN, :WIN] - o[WIN:, WIN:]
    bi = o[:WIN, WIN:] + o[WIN:, :WIN]
    rh, rl = split(br)
    ih, il = split(bi)
    mid = slice(PAD, PAD + BLK)
    o = dot3(rows(rh[mid], ih[mid]), rows(rl[mid], il[mid]), lanes(rh, ih), lanes(rl, il))
    return o[:BLK, :WIN] - o[BLK:, WIN:], o[:BLK, WIN:] + o[BLK:, :WIN]


def upper_half():
    return lax.broadcasted_iota(jnp.int32, (8, BLK), 0) >= 4


def pack_last(buf, xr, xi):
    buf[0:32, :] = xr[96:128]
    buf[32:64, :] = xi[96:128]
    buf[64:72, :] = jnp.where(upper_half(), xr[88:96], pltpu.roll(xi[88:96], 4, 0))


def pack_first(buf, xr, xi):
    buf[0:32, :] = xr[0:32]
    buf[32:64, :] = xi[0:32]
    buf[64:72, :] = jnp.where(upper_half(), pltpu.roll(xi[32:40], 4, 0), xr[32:40])


def kernel(
    n_src, n_rcv, n_freq,
    u_ref, op_ref, vel_ref, idx_ref, wgt_ref, perm_ref,
    out_ref, img_ref,
    tab, raw, mix, crw, cw, w_op, s_op, xh, xl,
    to_l, to_r, from_l, from_r, to_u, to_d, from_u, from_d,
    img_mine, img_all, img_sum, img_got,
    r_send, r_recv, s_send, s_recv, f_send, f_recv, g_send, g_recv,
):
    h = lax.axis_index("src")
    c = lax.axis_index("rcv")
    f = lax.axis_index("freq")
    n_blk = out_ref.shape[2] // BLK
    n_tile = vel_ref.shape[0]
    n_vel = idx_ref.shape[0]
    has_l, has_r = c > 0, c < n_rcv - 1
    has_u, has_d = h > 0, h < n_src - 1
    owner = h == c // n_blk

    barrier = pltpu.get_barrier_semaphore()

    @pl.when(has_l)
    def _():
        pl.semaphore_signal(barrier, inc=1, device_id={"rcv": c - 1}, device_id_type=MESH)

    @pl.when(has_r)
    def _():
        pl.semaphore_signal(barrier, inc=1, device_id={"rcv": c + 1}, device_id_type=MESH)

    for d in range(1, n_src):
        pl.semaphore_signal(barrier, inc=1, device_id={"src": lax.rem(h + d, n_src)}, device_id_type=MESH)
    for d in range(1, n_freq):
        pl.semaphore_signal(barrier, inc=1, device_id={"freq": lax.rem(f + d, n_freq)}, device_id_type=MESH)

    def pack_chunk(q, _):
        r = pl.multiple_of(q * BLK, BLK)
        tr = u_ref[0, 0, pl.ds(r, BLK), :].T
        ti = u_ref[1, 0, pl.ds(r, BLK), :].T
        pack_first(to_l.at[q], tr, ti)
        pack_last(to_r.at[q], tr, ti)
        return 0

    lax.fori_loop(0, n_blk, pack_chunk, 0)

    @pl.when(jnp.logical_not(has_l))
    def _():
        from_l[...] = jnp.zeros_like(from_l)

    @pl.when(jnp.logical_not(has_r))
    def _():
        from_r[...] = jnp.zeros_like(from_r)

    @pl.when(jnp.logical_not(has_u))
    def _():
        from_u[...] = jnp.zeros_like(from_u)

    @pl.when(jnp.logical_not(has_d))
    def _():
        from_d[...] = jnp.zeros_like(from_d)

    count = has_l.astype(jnp.int32) + has_r.astype(jnp.int32) + (n_src - 1) + (n_freq - 1)
    pl.semaphore_wait(barrier, count)

    def copy_l(q):
        return pltpu.make_async_remote_copy(
            to_l.at[q], from_r.at[q], r_send.at[0, q], r_recv.at[0, q],
            device_id={"rcv": jnp.maximum(c - 1, 0)}, device_id_type=MESH)

    def copy_r(q):
        return pltpu.make_async_remote_copy(
            to_r.at[q], from_l.at[q], r_send.at[1, q], r_recv.at[1, q],
            device_id={"rcv": jnp.minimum(c + 1, n_rcv - 1)}, device_id_type=MESH)

    def copy_u():
        return pltpu.make_async_remote_copy(
            to_u, from_d, s_send.at[0], s_recv.at[0],
            device_id={"src": jnp.maximum(h - 1, 0)}, device_id_type=MESH)

    def copy_d():
        return pltpu.make_async_remote_copy(
            to_d, from_u, s_send.at[1], s_recv.at[1],
            device_id={"src": jnp.minimum(h + 1, n_src - 1)}, device_id_type=MESH)

    order = [0, n_blk - 1] + list(range(1, n_blk - 1))
    for q in order:
        @pl.when(has_l)
        def _():
            copy_l(q).start()

        @pl.when(has_r)
        def _():
            copy_r(q).start()

    tab[...] = jnp.zeros_like(tab)
    tab[:, :, 0:TAPS] = op_ref[...]
    slot = perm_ref[0]
    for v in range(n_vel):
        i = idx_ref[v, slot]
        wgt = wgt_ref[v, slot]
        for p in range(2):
            raw[p, v:v + 1, :] = tab[p, pl.ds(i, 1), :] * (1.0 - wgt) + tab[p, pl.ds(i + 1, 1), :] * wgt
    for p in range(2):
        wide = lanes(raw[p], jnp.zeros((n_vel, BLK), F32))
        mix[:, WIN * p:WIN * (p + 1)] = pltpu.roll(wide, WIN - TAPS // 2, 1)

    def taps_at(dst, first_tile):
        def one(t, _):
            g = first_tile + t
            inside = jnp.logical_and(g >= 0, g < n_tile).astype(F32)
            v = vel_ref[jnp.clip(g, 0, n_tile - 1)]
            line = mix[pl.ds(v, 1), :] * inside
            dst[pl.ds(pl.multiple_of(t * TILE, TILE), TILE), :] = jnp.broadcast_to(line, (TILE, 2 * WIN))
            return 0
        lax.fori_loop(0, dst.shape[0] // TILE, one, 0)

    taps_at(crw, (c * BLK - PAD) // TILE)
    mr, mi = operator_block(crw[:, :WIN], crw[:, WIN:])
    sub = upper_half()
    pieces = []
    for m in (mr, mi):
        mt = lanes(m[:, :BLK], m[:, BLK:])
        t = rows(mt[:, :BLK].T, mt[:, BLK:].T)
        pieces.append(jnp.concatenate([
            t[PAD:PAD + BLK], t[32:64], t[192:224], jnp.where(sub, t[24:32], t[224:232]),
            jnp.zeros((BLK - SLAB, BLK), F32)], axis=0))
    wh, wl = split(lanes(pieces[0], pieces[1]))
    w_op[0:WIN, :] = wh
    w_op[WIN:2 * WIN, :] = wh
    w_op[2 * WIN:, :] = wl

    def receivers(q):
        @pl.when(has_r)
        def _():
            copy_l(q).wait_recv()

        @pl.when(has_l)
        def _():
            copy_r(q).wait_recv()

        l8, r8 = from_l[q, 64:72, :], from_r[q, 64:72, :]
        zero = jnp.zeros((BLK - SLAB, BLK), F32)
        hr = jnp.concatenate([from_l[q, 0:32, :], from_r[q, 0:32, :], jnp.where(sub, l8, r8), zero], axis=0).T
        hi = jnp.concatenate([from_l[q, 32:64, :], from_r[q, 32:64, :],
                              pltpu.roll(jnp.where(sub, r8, l8), 4, 0), zero], axis=0).T
        at = slice(q * BLK, (q + 1) * BLK)
        a = rows(lanes(u_ref[0, 0, at, :], hr), lanes(u_ref[1, 0, at, :], hi))
        ah, al = split(a)
        o = jnp.dot(jnp.concatenate([ah, al, ah], axis=1), w_op[...], preferred_element_type=F32)
        xr = o[:BLK, :BLK] - o[BLK:, BLK:]
        xi = o[:BLK, BLK:] + o[BLK:, :BLK]
        xhi, xlo = split(lanes(xr, xi))
        xh[PAD + q * BLK:PAD + (q + 1) * BLK, :] = xhi
        xl[PAD + q * BLK:PAD + (q + 1) * BLK, :] = xlo
        return xr, xi

    xr, xi = receivers(order[0])
    pack_first(to_u, xr, xi)

    @pl.when(has_u)
    def _():
        copy_u().start()

    xr, xi = receivers(order[1])
    pack_last(to_d, xr, xi)

    @pl.when(has_d)
    def _():
        copy_d().start()

    taps_at(cw, (h * n_blk * BLK - PAD) // TILE)

    def make_source_operator(b, _):
        r = pl.multiple_of(b * BLK, BLK)
        sr, si = operator_block(cw[pl.ds(r, WIN), :WIN], cw[pl.ds(r, WIN), WIN:])
        sh, sl = split(rows(sr, si))
        s_op[b, :, :WIN] = sh
        s_op[b, :, WIN:] = sl
        return 0

    lax.fori_loop(0, n_blk, make_source_operator, 0)

    for q in order[2:]:
        receivers(q)

    @pl.when(has_u)
    def _():
        copy_d().wait_recv()

    @pl.when(has_d)
    def _():
        copy_u().wait_recv()

    zero = jnp.zeros((8, BLK), F32)
    u8, d8 = from_u[64:72, :], from_d[64:72, :]
    pad = jnp.zeros((24, 2 * BLK), F32)
    top = jnp.concatenate([
        pad,
        lanes(jnp.where(sub, u8, zero), pltpu.roll(jnp.where(sub, zero, u8), 4, 0)),
        lanes(from_u[0:32, :], from_u[32:64, :])], axis=0)
    low = jnp.concatenate([
        lanes(from_d[0:32, :], from_d[32:64, :]),
        lanes(jnp.where(sub, zero, d8), pltpu.roll(jnp.where(sub, d8, zero), 4, 0)),
        pad], axis=0)
    end = PAD + n_blk * BLK
    xh[0:PAD, :], xl[0:PAD, :] = split(top)
    xh[end:end + PAD, :], xl[end:end + PAD, :] = split(low)

    def sources(b, _):
        r = pl.multiple_of(b * BLK, BLK)
        bh, bl = xh[pl.ds(r, WIN), :], xl[pl.ds(r, WIN), :]
        o = dot3(s_op[b, :, :WIN], s_op[b, :, WIN:], bh, bl)
        out_ref[0, 0, pl.ds(r, BLK), :] = o[:BLK, :BLK] - o[BLK:, BLK:]
        out_ref[1, 0, pl.ds(r, BLK), :] = o[:BLK, BLK:] + o[BLK:, :BLK]
        return 0

    lax.fori_loop(0, n_blk, sources, 0)

    def copy_f(d):
        return pltpu.make_async_remote_copy(
            img_mine, img_all.at[f], f_send.at[d - 1], f_recv.at[d - 1],
            device_id={"freq": lax.rem(f + d, n_freq)}, device_id_type=MESH)

    def copy_g(d):
        return pltpu.make_async_remote_copy(
            img_sum, img_got, g_send.at[d - 1], g_recv,
            device_id={"src": lax.rem(h + d, n_src)}, device_id_type=MESH)

    @pl.when(owner)
    def _():
        r = pl.multiple_of(lax.rem(c, n_blk) * BLK, BLK)
        block = out_ref[0, 0, pl.ds(r, BLK), :]
        on = lax.broadcasted_iota(jnp.int32, (BLK, BLK), 0) == lax.broadcasted_iota(jnp.int32, (BLK, BLK), 1)
        diag = jnp.broadcast_to(jnp.sum(jnp.where(on, block, 0.0), axis=0, keepdims=True), (8, BLK))
        img_mine[...] = diag
        img_all[f] = diag
        for d in range(1, n_freq):
            copy_f(d).start()
        for d in range(1, n_freq):
            copy_f(d).wait()
        total = img_all[0]
        for i in range(1, n_freq):
            total = total + img_all[i]
        img_sum[...] = total
        img_ref[...] = total[0:1]
        for d in range(1, n_src):
            copy_g(d).start()
        for d in range(1, n_src):
            copy_g(d).wait_send()

    @pl.when(jnp.logical_not(owner))
    def _():
        copy_g(1).wait_recv()
        img_ref[...] = img_got[0:1, :]

    for q in order:
        @pl.when(has_l)
        def _():
            copy_l(q).wait_send()

        @pl.when(has_r)
        def _():
            copy_r(q).wait_send()

    @pl.when(has_u)
    def _():
        copy_u().wait_send()

    @pl.when(has_d)
    def _():
        copy_d().wait_send()


def body(n_src, n_rcv, n_freq, wavefield, op_table, vel_index, interp_index, interp_weight, freq_perm):
    n_blk = wavefield.shape[2] // BLK
    n_tab, n_vel = op_table.shape[1], interp_index.shape[0]
    vmem = pl.BlockSpec(memory_space=pltpu.VMEM)
    smem = pl.BlockSpec(memory_space=pltpu.SMEM)
    dma = pltpu.SemaphoreType.DMA
    slabs = [pltpu.VMEM((n_blk, SLAB, BLK), F32)] * 4 + [pltpu.VMEM((SLAB, BLK), F32)] * 4
    sunk, image = pl.pallas_call(
        functools.partial(kernel, n_src, n_rcv, n_freq),
        out_shape=(jax.ShapeDtypeStruct(wavefield.shape, F32), jax.ShapeDtypeStruct((1, BLK), F32)),
        in_specs=[vmem, vmem, smem, smem, smem, smem],
        out_specs=(vmem, vmem),
        scratch_shapes=[
            pltpu.VMEM((2, n_tab, BLK), F32),
            pltpu.VMEM((2, n_vel, BLK), F32),
            pltpu.VMEM((n_vel, 2 * WIN), F32),
            pltpu.VMEM((WIN, 2 * WIN), F32),
            pltpu.VMEM((2 * PAD + n_blk * BLK, 2 * WIN), F32),
            pltpu.VMEM((3 * WIN, WIN), BF),
            pltpu.VMEM((n_blk, WIN, 2 * WIN), BF),
            pltpu.VMEM((2 * PAD + n_blk * BLK, WIN), BF),
            pltpu.VMEM((2 * PAD + n_blk * BLK, WIN), BF),
            *slabs,
            pltpu.VMEM((8, BLK), F32),
            pltpu.VMEM((n_freq, 8, BLK), F32),
            pltpu.VMEM((8, BLK), F32),
            pltpu.VMEM((8, BLK), F32),
            dma((2, n_blk)), dma((2, n_blk)), dma((2,)), dma((2,)),
            dma((max(n_freq - 1, 1),)), dma((max(n_freq - 1, 1),)), dma((max(n_src - 1, 1),)), dma,
        ],
        compiler_params=pltpu.CompilerParams(collective_id=0, has_side_effects=True),
        name="depth_step",
    )(wavefield, op_table, vel_index, interp_index, interp_weight, freq_perm)
    return sunk, image.reshape(BLK)


def solution(mesh):
    sizes = [mesh.shape[a] for a in ("src", "rcv", "freq")]
    in_specs = (P(None, "freq", "src", "rcv"), P(), P(), P(), P(), P("freq"))
    out_specs = (P(None, "freq", "src", "rcv"), P("rcv"))
    return jax.shard_map(functools.partial(body, *sizes), mesh=mesh, in_specs=in_specs, out_specs=out_specs,
                         check_vma=False)
```

```python
import functools

import jax
import jax.numpy as jnp
from jax import lax
from jax.experimental import pallas as pl
from jax.experimental.pallas import tpu as pltpu
from jax.sharding import PartitionSpec as P

MESH = pl.DeviceIdType.MESH
F32 = jnp.float32
BF = jnp.bfloat16
TILE = 16
TAPS = 19
HALO = 36
BLK = 128
PAD = 64
WIN = 256
HOLD = 2
SLAB = 72


def split(x):
    hi = x.astype(BF)
    return hi, (x - hi.astype(F32)).astype(BF)


def dot3(ah, al, bh, bl):
    a = jnp.concatenate([ah, al, ah], axis=1)
    b = jnp.concatenate([bh, bh, bl], axis=0)
    return jnp.dot(a, b, preferred_element_type=F32)


def rows(a, b):
    return jnp.concatenate([a, b], axis=0)


def lanes(a, b):
    return jnp.concatenate([a, b], axis=1)


def operator_block(cr, ci):
    ar = pltpu.roll(cr, 0, 1, stride=1, stride_axis=0)
    ai = pltpu.roll(ci, 0, 1, stride=1, stride_axis=0)
    rh, rl = split(ar)
    ih, il = split(ai)
    near = slice(PAD // 2, WIN - PAD // 2)
    o = dot3(rows(rh[near], ih[near]), rows(rl[near], il[near]), lanes(rh, ih), lanes(rl, il))
    n = WIN - PAD
    br = o[:n, :WIN] - o[n:, WIN:]
    bi = o[:n, WIN:] + o[n:, :WIN]
    rh, rl = split(br)
    ih, il = split(bi)
    mid = slice(PAD // 2, PAD // 2 + BLK)
    edge = jnp.zeros((PAD // 2, 2 * WIN), BF)
    bh = jnp.concatenate([edge, lanes(rh, ih), edge], axis=0)
    bl = jnp.concatenate([edge, lanes(rl, il), edge], axis=0)
    o = dot3(rows(rh[mid], ih[mid]), rows(rl[mid], il[mid]), bh, bl)
    return o[:BLK, :WIN] - o[BLK:, WIN:], o[:BLK, WIN:] + o[BLK:, :WIN]


def upper_half():
    return lax.broadcasted_iota(jnp.int32, (8, BLK), 0) >= 4


def pack_last(buf, xr, xi):
    buf[0:32, :] = xr[96:128]
    buf[32:64, :] = xi[96:128]
    buf[64:72, :] = jnp.where(upper_half(), xr[88:96], pltpu.roll(xi[88:96], 4, 0))


def pack_first(buf, xr, xi):
    buf[0:32, :] = xr[0:32]
    buf[32:64, :] = xi[0:32]
    buf[64:72, :] = jnp.where(upper_half(), pltpu.roll(xi[32:40], 4, 0), xr[32:40])


def kernel(
    n_src, n_rcv, n_freq,
    u_ref, op_ref, vel_ref, idx_ref, wgt_ref, perm_ref,
    out_ref, img_ref,
    raw, turn, mix, crw, cw, w_op, s_op, xh, xl,
    to_l, to_r, from_l, from_r, to_u, to_d, from_u, from_d,
    img_mine, img_all,
    r_send, r_recv, s_send, s_recv, f_send, f_recv, known_u, known_d,
):
    h = lax.axis_index("src")
    c = lax.axis_index("rcv")
    f = lax.axis_index("freq")
    n_blk = out_ref.shape[2] // BLK
    n_tile = vel_ref.shape[0]
    n_tab = op_ref.shape[2]
    n_vel = idx_ref.shape[1]
    has_l, has_r = c > 0, c < n_rcv - 1
    has_u, has_d = h > 0, h < n_src - 1
    owner = h == c // n_blk
    quarter = lax.rem(c, n_blk)

    def to(axis, index):
        return dict(device_id={axis: index}, device_id_type=MESH)

    up, down = to("src", jnp.maximum(h - 1, 0)), to("src", jnp.minimum(h + 1, n_src - 1))
    left, right = to("rcv", jnp.maximum(c - 1, 0)), to("rcv", jnp.minimum(c + 1, n_rcv - 1))

    def each(pairs):
        for cond, act in pairs:
            pl.when(cond)(act)

    barrier = pltpu.get_barrier_semaphore()
    each([
        (has_l, lambda: pl.semaphore_signal(barrier, 1, **left)),
        (has_r, lambda: pl.semaphore_signal(barrier, 1, **right)),
        (has_u, lambda: pl.semaphore_signal(barrier, 1, **up)),
        (has_d, lambda: pl.semaphore_signal(barrier, 1, **down)),
    ])
    for d in range(1, n_freq):
        pl.semaphore_signal(barrier, 1, **to("freq", lax.rem(f + d, n_freq)))

    n_mid = n_blk - 1

    def chunk_start(p, col):
        back = lax.rem(col, n_blk) >= n_blk // 2
        return pl.multiple_of(PAD + BLK * jnp.where(back, n_mid - p, p - 1), PAD)

    def part_lines(part, p, col):
        if p == 0:
            last = u_ref.shape[2] - PAD
            return rows(u_ref[part, 0, 0:PAD, :], u_ref[part, 0, last:last + PAD, :])
        return u_ref[part, 0, pl.ds(chunk_start(p, col), BLK), :]

    def pack(p):
        pack_first(to_l.at[p], part_lines(0, p, jnp.maximum(c - 1, 0)).T, part_lines(1, p, jnp.maximum(c - 1, 0)).T)
        pack_last(to_r.at[p], part_lines(0, p, c + 1).T, part_lines(1, p, c + 1).T)

    def copy_l(p):
        return pltpu.make_async_remote_copy(to_l.at[p], from_r.at[p], r_send.at[0, p], r_recv.at[0, p], **left)

    def copy_r(p):
        return pltpu.make_async_remote_copy(to_r.at[p], from_l.at[p], r_send.at[1, p], r_recv.at[1, p], **right)

    def copy_u():
        return pltpu.make_async_remote_copy(to_u, from_d, s_send.at[0], s_recv.at[0], **up)

    def copy_d():
        return pltpu.make_async_remote_copy(to_d, from_u, s_send.at[1], s_recv.at[1], **down)

    def send(p):
        each([(has_l, lambda: copy_l(p).start()), (has_r, lambda: copy_r(p).start())])

    def clear(ref):
        ref[...] = jnp.zeros_like(ref)

    pack(0)
    pack(1)
    each([
        (jnp.logical_not(has_l), lambda: clear(from_l)),
        (jnp.logical_not(has_r), lambda: clear(from_r)),
        (jnp.logical_not(has_u), lambda: clear(from_u)),
        (jnp.logical_not(has_d), lambda: clear(from_d)),
    ])

    clear(raw)
    clear(turn)
    raw[0, 0:TAPS, :] = op_ref[:, 0, :]
    raw[1, 0:TAPS, :] = op_ref[:, 1, :]
    slot = perm_ref[0]
    row = idx_ref[pl.ds(slot, 1), :]
    wgt = wgt_ref[pl.ds(slot, 1), :]
    line = lax.broadcasted_iota(jnp.int32, (n_tab, n_vel), 0)
    table = rows(raw[0], raw[1])
    hi, rest = table.astype(BF), table - table.astype(BF).astype(F32)
    mid, low = split(rest)
    table = jnp.concatenate([hi, mid, low], axis=1)

    def picked(which):
        one = (line == which).astype(F32).astype(BF)
        return jnp.dot(table, jnp.concatenate([one, one, one], axis=0), preferred_element_type=F32)

    turn[0:64, 0:n_vel] = picked(row) * (1.0 - wgt) + picked(row + 1) * wgt
    turned = turn[...].T[0:n_vel]
    few = lax.broadcasted_iota(jnp.int32, (n_vel, BLK), 1) < 32
    none = jnp.zeros((n_vel, BLK), F32)
    for p in range(2):
        part = jnp.where(few, pltpu.roll(turned, (BLK - 32 * p) % BLK, 1), 0.0)
        mix[:, WIN * p:WIN * (p + 1)] = pltpu.roll(lanes(part, none), WIN - TAPS // 2, 1)

    ones = lambda cond: cond.astype(jnp.int32)
    pl.semaphore_wait(barrier, ones(has_l) + ones(has_r) + ones(has_u) + ones(has_d) + (n_freq - 1))
    for p in range(HOLD):
        send(p)

    def tell(t):
        each([
            (has_d if t == 0 else jnp.logical_and(has_d, h >= t), lambda: pl.semaphore_signal(known_u.at[t], 1, **down)),
            (has_u if t == 0 else jnp.logical_and(has_u, h <= n_src - 1 - t),
             lambda: pl.semaphore_signal(known_d.at[t], 1, **up)),
        ])

    def learn(t):
        each([
            (h >= t + 1, lambda: pl.semaphore_wait(known_u.at[t], 1)),
            (h <= n_src - 2 - t, lambda: pl.semaphore_wait(known_d.at[t], 1)),
        ])

    tell(0)
    for p in range(2, n_blk):
        pack(p)

    def taps_at(dst, first_tile):
        def one(t, _):
            g = first_tile + t
            inside = jnp.logical_and(g >= 0, g < n_tile).astype(F32)
            v = vel_ref[jnp.clip(g, 0, n_tile - 1)]
            line = mix[pl.ds(v, 1), :] * inside
            dst[pl.ds(pl.multiple_of(t * TILE, TILE), TILE), :] = jnp.broadcast_to(line, (TILE, 2 * WIN))
            return 0
        lax.fori_loop(0, dst.shape[0] // TILE, one, 0)

    sub = upper_half()
    taps_at(crw, (c * BLK - PAD) // TILE)
    mr, mi = operator_block(crw[:, :WIN], crw[:, WIN:])
    pieces = []
    for m in (mr, mi):
        t = rows(m[:, :BLK].T, m[:, BLK:].T)
        pieces.append(jnp.concatenate([
            t[PAD:PAD + BLK], t[32:64], t[192:224], jnp.where(sub, t[24:32], t[224:232]),
            jnp.zeros((BLK - SLAB, BLK), F32)], axis=0))
    wh, wl = split(lanes(pieces[0], pieces[1]))
    w_op[0:WIN, :] = wh
    w_op[WIN:2 * WIN, :] = wh
    w_op[2 * WIN:, :] = wl
    taps_at(cw, (h * n_blk * BLK - PAD) // TILE)

    def make_source_operator(k):
        b = lax.rem(quarter + k, n_blk)
        r = pl.multiple_of(b * BLK, BLK)
        sr, si = operator_block(cw[pl.ds(r, WIN), :WIN], cw[pl.ds(r, WIN), WIN:])
        sh, sl = split(rows(sr, si))
        s_op[b, :, :WIN] = sh
        s_op[b, :, WIN:] = sl

    def receivers(p):
        each([(has_r, lambda: copy_l(p).wait_recv()), (has_l, lambda: copy_r(p).wait_recv())])
        l8, r8 = from_l[p, 64:72, :], from_r[p, 64:72, :]
        zero = jnp.zeros((BLK - SLAB, BLK), F32)
        hr = jnp.concatenate([from_l[p, 0:32, :], from_r[p, 0:32, :], jnp.where(sub, l8, r8), zero], axis=0).T
        hi = jnp.concatenate([from_l[p, 32:64, :], from_r[p, 32:64, :],
                              pltpu.roll(jnp.where(sub, r8, l8), 4, 0), zero], axis=0).T
        ah, al = split(rows(lanes(part_lines(0, p, c), hr), lanes(part_lines(1, p, c), hi)))
        o = jnp.dot(jnp.concatenate([ah, al, ah], axis=1), w_op[...], preferred_element_type=F32)
        xr = o[:BLK, :BLK] - o[BLK:, BLK:]
        xi = o[:BLK, BLK:] + o[BLK:, :BLK]
        xhi, xlo = split(lanes(xr, xi))
        if p == 0:
            end = n_blk * BLK
            xh[PAD:2 * PAD, :], xl[PAD:2 * PAD, :] = xhi[:PAD], xlo[:PAD]
            xh[end:end + PAD, :], xl[end:end + PAD, :] = xhi[PAD:], xlo[PAD:]
            pack_first(to_u, xr, xi)
            pack_last(to_d, xr, xi)
        else:
            at = pl.ds(chunk_start(p, c) + PAD, BLK)
            xh[at, :] = xhi
            xl[at, :] = xlo

    make_source_operator(0)
    receivers(0)
    each([(has_u, lambda: copy_u().start()), (has_d, lambda: copy_d().start())])
    for p in range(HOLD, n_blk):
        send(p)
    for t in range(1, n_src - 1):
        learn(t - 1)
        tell(t)
    make_source_operator(1)
    receivers(1)
    make_source_operator(2)
    receivers(2)

    each([(has_u, lambda: copy_d().wait_recv()), (has_d, lambda: copy_u().wait_recv())])
    zero = jnp.zeros((8, BLK), F32)
    u8, d8 = from_u[64:72, :], from_d[64:72, :]
    pad = jnp.zeros((24, 2 * BLK), F32)
    top = jnp.concatenate([
        pad,
        lanes(jnp.where(sub, u8, zero), pltpu.roll(jnp.where(sub, zero, u8), 4, 0)),
        lanes(from_u[0:32, :], from_u[32:64, :])], axis=0)
    low = jnp.concatenate([
        lanes(from_d[0:32, :], from_d[32:64, :]),
        lanes(jnp.where(sub, zero, d8), pltpu.roll(jnp.where(sub, d8, zero), 4, 0)),
        pad], axis=0)
    end = PAD + n_blk * BLK
    xh[0:PAD, :], xl[0:PAD, :] = split(top)
    xh[end:end + PAD, :], xl[end:end + PAD, :] = split(low)

    def sources(k):
        b = lax.rem(quarter + k, n_blk)
        r = pl.multiple_of(b * BLK, BLK)
        o = dot3(s_op[b, :, :WIN], s_op[b, :, WIN:], xh[pl.ds(r, WIN), :], xl[pl.ds(r, WIN), :])
        yr = o[:BLK, :BLK] - o[BLK:, BLK:]
        out_ref[0, 0, pl.ds(r, BLK), :] = yr
        out_ref[1, 0, pl.ds(r, BLK), :] = o[:BLK, BLK:] + o[BLK:, :BLK]
        return yr

    n_peer = n_src * n_freq

    def copy_image(d):
        e = lax.rem(h * n_freq + f + d, n_peer)
        return pltpu.make_async_remote_copy(
            img_mine, img_all.at[f], f_send.at[d], f_recv.at[f],
            device_id={"src": e // n_freq, "freq": lax.rem(e, n_freq)}, device_id_type=MESH)

    yr = sources(0)
    learn(n_src - 2)

    @pl.when(owner)
    def _():
        on = lax.broadcasted_iota(jnp.int32, (BLK, BLK), 0) == lax.broadcasted_iota(jnp.int32, (BLK, BLK), 1)
        diag = jnp.broadcast_to(jnp.sum(jnp.where(on, yr, 0.0), axis=0, keepdims=True), (8, BLK))
        img_mine[...] = diag
        img_all[f] = diag

        def start(d, _):
            copy_image(d).start()
            return 0
        lax.fori_loop(1, n_peer, start, 0)

    make_source_operator(3)
    receivers(3)
    for k in range(1, n_blk):
        sources(k)

    def got(i, _):
        @pl.when(jnp.logical_not(jnp.logical_and(owner, f == i)))
        def _():
            pltpu.make_async_remote_copy(
                img_mine, img_all.at[i], f_send.at[0], f_recv.at[i],
                device_id={"src": h, "freq": f}, device_id_type=MESH).wait_recv()
        return 0
    lax.fori_loop(0, n_freq, got, 0)
    total = img_all[0]
    for i in range(1, n_freq):
        total = total + img_all[i]
    img_ref[...] = total[0:1]

    @pl.when(owner)
    def _():
        def sent(d, _):
            copy_image(d).wait_send()
            return 0
        lax.fori_loop(1, n_peer, sent, 0)

    for p in range(n_blk):
        each([(has_l, lambda: copy_l(p).wait_send()), (has_r, lambda: copy_r(p).wait_send())])
    each([(has_u, lambda: copy_u().wait_send()), (has_d, lambda: copy_d().wait_send())])


def body(n_src, n_rcv, n_freq, wavefield, op_table, vel_index, interp_index, interp_weight, freq_perm):
    n_blk = wavefield.shape[2] // BLK
    n_tab, n_vel = op_table.shape[1], interp_index.shape[0]
    vmem = pl.BlockSpec(memory_space=pltpu.VMEM)
    smem = pl.BlockSpec(memory_space=pltpu.SMEM)
    dma, flag = pltpu.SemaphoreType.DMA, pltpu.SemaphoreType.REGULAR
    slabs = [pltpu.VMEM((n_blk, SLAB, BLK), F32)] * 4 + [pltpu.VMEM((SLAB, BLK), F32)] * 4
    length = 2 * PAD + n_blk * BLK
    sunk, image = pl.pallas_call(
        functools.partial(kernel, n_src, n_rcv, n_freq),
        out_shape=(pltpu.VMEM(wavefield.shape, F32), pltpu.VMEM((1, BLK), F32)),
        in_specs=[vmem, vmem, smem, vmem, vmem, smem],
        out_specs=(vmem, vmem),
        scratch_shapes=[
            pltpu.VMEM((2, 32, n_tab), F32),
            pltpu.VMEM((BLK, BLK), F32),
            pltpu.VMEM((n_vel, 2 * WIN), F32),
            pltpu.VMEM((WIN, 2 * WIN), F32),
            pltpu.VMEM((length, 2 * WIN), F32),
            pltpu.VMEM((3 * WIN, WIN), BF),
            pltpu.VMEM((n_blk, WIN, 2 * WIN), BF),
            pltpu.VMEM((length, WIN), BF),
            pltpu.VMEM((length, WIN), BF),
            *slabs,
            pltpu.VMEM((8, BLK), F32),
            pltpu.VMEM((n_freq, 8, BLK), F32),
            dma((2, n_blk)), dma((2, n_blk)), dma((2,)), dma((2,)),
            dma((n_src * n_freq,)), dma((n_freq,)), flag((n_src - 1,)), flag((n_src - 1,)),
        ],
        compiler_params=pltpu.CompilerParams(collective_id=0, has_side_effects=True),
        name="depth_step",
    )(wavefield, jnp.transpose(op_table, (2, 0, 1)), vel_index, interp_index.T, interp_weight.T, freq_perm)
    return sunk, image.reshape(BLK)


def solution(mesh):
    sizes = [mesh.shape[a] for a in ("src", "rcv", "freq")]
    in_specs = (P(None, "freq", "src", "rcv"), P(), P(), P(), P(), P("freq"))
    out_specs = (P(None, "freq", "src", "rcv"), P("rcv"))
    return jax.shard_map(functools.partial(body, *sizes), mesh=mesh, in_specs=in_specs, out_specs=out_specs,
                         check_vma=False)
```

```python
import functools

import jax
import jax.numpy as jnp
from jax import lax
from jax.experimental import pallas as pl
from jax.experimental.pallas import tpu as pltpu
from jax.sharding import PartitionSpec as P

MESH = pl.DeviceIdType.MESH
F32 = jnp.float32
BF = jnp.bfloat16
TILE = 16
TAPS = 19
HALO = 36
BLK = 128
PAD = 64
WIN = 256
HOLD = 2
SLAB = 72


def split(x):
    hi = x.astype(BF)
    return hi, (x - hi.astype(F32)).astype(BF)


def dot3(ah, al, bh, bl):
    a = jnp.concatenate([ah, al, ah], axis=1)
    b = jnp.concatenate([bh, bh, bl], axis=0)
    return jnp.dot(a, b, preferred_element_type=F32)


def rows(a, b):
    return jnp.concatenate([a, b], axis=0)


def lanes(a, b):
    return jnp.concatenate([a, b], axis=1)


def operator_blocks(taps):
    near, mid = slice(PAD // 2, WIN - PAD // 2), slice(PAD, PAD + BLK)

    def parts(re, im):
        return [split(re), split(im), split(re + im)]

    def products(three, at):
        return [dot3(h[at], l[at], h, l) for h, l in three]

    def whole(x):
        edge = jnp.zeros((PAD // 2, WIN), F32)
        return jnp.concatenate([edge, x, edge], axis=0)

    ones = [[pltpu.roll(x, 0, 1, stride=1, stride_axis=0) for x in pair] for pair in taps]
    ones = [parts(*pair) for pair in ones]
    twos = [products(three, near) for three in ones]
    twos = [parts(whole(p - q), whole(r - p - q)) for p, q, r in twos]
    fours = [products(three, mid) for three in twos]
    return [(p - q, r - p - q) for p, q, r in fours]


def upper_half():
    return lax.broadcasted_iota(jnp.int32, (8, BLK), 0) >= 4


def pack_last(buf, xr, xi):
    buf[0:32, :] = xr[96:128]
    buf[32:64, :] = xi[96:128]
    buf[64:72, :] = jnp.where(upper_half(), xr[88:96], pltpu.roll(xi[88:96], 4, 0))


def pack_first(buf, xr, xi):
    buf[0:32, :] = xr[0:32]
    buf[32:64, :] = xi[0:32]
    buf[64:72, :] = jnp.where(upper_half(), pltpu.roll(xi[32:40], 4, 0), xr[32:40])


def kernel(
    n_src, n_rcv, n_freq,
    u_any, op_any, vel_any, idx_any, wgt_any, perm_ref,
    out_ref, img_ref,
    raw, turn, mix, crw, cw, w_op, s_op, xh, xl,
    to_l, to_r, from_l, from_r, to_u, to_d, from_u, from_d,
    img_mine, img_all, u_ref, op_ref, vel_ref, idx_ref, wgt_ref,
    in_sem, r_send, r_recv, s_send, s_recv, f_send, f_recv, known_u, known_d,
):
    h = lax.axis_index("src")
    c = lax.axis_index("rcv")
    f = lax.axis_index("freq")
    n_blk = out_ref.shape[2] // BLK
    n_tile = vel_any.shape[0]
    n_tab = op_any.shape[2]
    n_vel = idx_any.shape[1]
    has_l, has_r = c > 0, c < n_rcv - 1
    has_u, has_d = h > 0, h < n_src - 1
    owner = h == c // n_blk
    quarter = lax.rem(c, n_blk)

    def to(axis, index):
        return dict(device_id={axis: index}, device_id_type=MESH)

    up, down = to("src", jnp.maximum(h - 1, 0)), to("src", jnp.minimum(h + 1, n_src - 1))
    left, right = to("rcv", jnp.maximum(c - 1, 0)), to("rcv", jnp.minimum(c + 1, n_rcv - 1))

    def each(pairs):
        for cond, act in pairs:
            pl.when(cond)(act)

    barrier = pltpu.get_barrier_semaphore()
    each([
        (has_l, lambda: pl.semaphore_signal(barrier, 1, **left)),
        (has_r, lambda: pl.semaphore_signal(barrier, 1, **right)),
        (has_u, lambda: pl.semaphore_signal(barrier, 1, **up)),
        (has_d, lambda: pl.semaphore_signal(barrier, 1, **down)),
    ])
    for d in range(1, n_freq):
        pl.semaphore_signal(barrier, 1, **to("freq", lax.rem(f + d, n_freq)))

    n_row = u_any.shape[2]

    def fetch_lines(part, at, sem):
        return pltpu.make_async_copy(u_any.at[part, 0, at, :], u_ref.at[part, 0, at, :], in_sem.at[sem])

    outer_lines = [
        fetch_lines(part, at, 2 * part + k)
        for part in range(2) for k, at in enumerate([pl.ds(0, PAD), pl.ds(n_row - PAD, PAD)])]
    inner_lines = [fetch_lines(part, pl.ds(PAD, n_row - 2 * PAD), 4 + part) for part in range(2)]
    tables = [
        pltpu.make_async_copy(src, dst, in_sem.at[6 + k])
        for k, (src, dst) in enumerate([(op_any, op_ref), (idx_any, idx_ref), (wgt_any, wgt_ref), (vel_any, vel_ref)])]
    for copy in outer_lines + tables + inner_lines:
        copy.start()

    n_mid = n_blk - 1

    def chunk_start(p, col):
        back = lax.rem(col, n_blk) >= n_blk // 2
        return pl.multiple_of(PAD + BLK * jnp.where(back, n_mid - p, p - 1), PAD)

    def part_lines(part, p, col):
        if p == 0:
            last = u_ref.shape[2] - PAD
            return rows(u_ref[part, 0, 0:PAD, :], u_ref[part, 0, last:last + PAD, :])
        return u_ref[part, 0, pl.ds(chunk_start(p, col), BLK), :]

    def pack(p):
        pack_first(to_l.at[p], part_lines(0, p, jnp.maximum(c - 1, 0)).T, part_lines(1, p, jnp.maximum(c - 1, 0)).T)
        pack_last(to_r.at[p], part_lines(0, p, c + 1).T, part_lines(1, p, c + 1).T)

    def copy_l(p):
        return pltpu.make_async_remote_copy(to_l.at[p], from_r.at[p], r_send.at[0, p], r_recv.at[0, p], **left)

    def copy_r(p):
        return pltpu.make_async_remote_copy(to_r.at[p], from_l.at[p], r_send.at[1, p], r_recv.at[1, p], **right)

    def copy_u():
        return pltpu.make_async_remote_copy(to_u, from_d, s_send.at[0], s_recv.at[0], **up)

    def copy_d():
        return pltpu.make_async_remote_copy(to_d, from_u, s_send.at[1], s_recv.at[1], **down)

    def send(p):
        each([(has_l, lambda: copy_l(p).start()), (has_r, lambda: copy_r(p).start())])

    def clear(ref):
        ref[...] = jnp.zeros_like(ref)

    each([
        (jnp.logical_not(has_l), lambda: clear(from_l)),
        (jnp.logical_not(has_r), lambda: clear(from_r)),
        (jnp.logical_not(has_u), lambda: clear(from_u)),
        (jnp.logical_not(has_d), lambda: clear(from_d)),
    ])

    for copy in outer_lines:
        copy.wait()
    pack(0)
    ones = lambda cond: cond.astype(jnp.int32)
    pl.semaphore_wait(barrier, ones(has_l) + ones(has_r) + ones(has_u) + ones(has_d) + (n_freq - 1))

    def tell(t):
        each([
            (has_d if t == 0 else jnp.logical_and(has_d, h >= t), lambda: pl.semaphore_signal(known_u.at[t], 1, **down)),
            (has_u if t == 0 else jnp.logical_and(has_u, h <= n_src - 1 - t),
             lambda: pl.semaphore_signal(known_d.at[t], 1, **up)),
        ])

    def learn(t):
        each([
            (h >= t + 1, lambda: pl.semaphore_wait(known_u.at[t], 1)),
            (h <= n_src - 2 - t, lambda: pl.semaphore_wait(known_d.at[t], 1)),
        ])

    tell(0)
    send(0)

    for copy in tables:
        copy.wait()
    clear(raw)
    clear(turn)
    raw[0, 0:TAPS, :] = op_ref[:, 0, :]
    raw[1, 0:TAPS, :] = op_ref[:, 1, :]
    slot = perm_ref[0]
    row = idx_ref[pl.ds(slot, 1), :]
    wgt = wgt_ref[pl.ds(slot, 1), :]
    line = lax.broadcasted_iota(jnp.int32, (n_tab, n_vel), 0)
    table = rows(raw[0], raw[1])
    hi, rest = table.astype(BF), table - table.astype(BF).astype(F32)
    mid, low = split(rest)
    table = jnp.concatenate([hi, mid, low], axis=1)

    def picked(which):
        one = (line == which).astype(F32).astype(BF)
        return jnp.dot(table, jnp.concatenate([one, one, one], axis=0), preferred_element_type=F32)

    turn[0:64, 0:n_vel] = picked(row) * (1.0 - wgt) + picked(row + 1) * wgt
    turned = turn[...].T[0:n_vel]
    few = lax.broadcasted_iota(jnp.int32, (n_vel, BLK), 1) < 32
    none = jnp.zeros((n_vel, BLK), F32)
    for p in range(2):
        part = jnp.where(few, pltpu.roll(turned, (BLK - 32 * p) % BLK, 1), 0.0)
        mix[:, WIN * p:WIN * (p + 1)] = pltpu.roll(lanes(part, none), WIN - TAPS // 2, 1)

    def taps_at(dst, first_tile):
        def one(t, _):
            g = first_tile + t
            inside = jnp.logical_and(g >= 0, g < n_tile).astype(F32)
            v = vel_ref[jnp.clip(g, 0, n_tile - 1)]
            line = mix[pl.ds(v, 1), :] * inside
            dst[pl.ds(pl.multiple_of(t * TILE, TILE), TILE), :] = jnp.broadcast_to(line, (TILE, 2 * WIN))
            return 0
        lax.fori_loop(0, dst.shape[0] // TILE, one, 0)

    for copy in inner_lines:
        copy.wait()
    for p in range(1, HOLD):
        pack(p)
        send(p)
    for p in range(HOLD, n_blk):
        pack(p)

    sub = upper_half()
    taps_at(crw, (c * BLK - PAD) // TILE)
    taps_at(cw, (h * n_blk * BLK - PAD) // TILE)

    def source_taps(k):
        r = pl.multiple_of(lax.rem(quarter + k, n_blk) * BLK, BLK)
        return cw[pl.ds(r, WIN), :WIN], cw[pl.ds(r, WIN), WIN:]

    def keep_source_operator(k, sr, si):
        b = lax.rem(quarter + k, n_blk)
        sh, sl = split(rows(sr, si))
        s_op[b, :, :WIN] = sh
        s_op[b, :, WIN:] = sl

    (mr, mi), first = operator_blocks([(crw[:, :WIN], crw[:, WIN:]), source_taps(0)])
    keep_source_operator(0, *first)
    pieces = []
    for m in (mr, mi):
        t = rows(m[:, :BLK].T, m[:, BLK:].T)
        pieces.append(jnp.concatenate([
            t[PAD:PAD + BLK], t[32:64], t[192:224], jnp.where(sub, t[24:32], t[224:232]),
            jnp.zeros((BLK - SLAB, BLK), F32)], axis=0))
    wh, wl = split(lanes(pieces[0], pieces[1]))
    w_op[0:WIN, :] = wh
    w_op[WIN:2 * WIN, :] = wh
    w_op[2 * WIN:, :] = wl

    def receivers(p):
        each([(has_r, lambda: copy_l(p).wait_recv()), (has_l, lambda: copy_r(p).wait_recv())])
        l8, r8 = from_l[p, 64:72, :], from_r[p, 64:72, :]
        zero = jnp.zeros((BLK - SLAB, BLK), F32)
        hr = jnp.concatenate([from_l[p, 0:32, :], from_r[p, 0:32, :], jnp.where(sub, l8, r8), zero], axis=0).T
        hi = jnp.concatenate([from_l[p, 32:64, :], from_r[p, 32:64, :],
                              pltpu.roll(jnp.where(sub, r8, l8), 4, 0), zero], axis=0).T
        ah, al = split(rows(lanes(part_lines(0, p, c), hr), lanes(part_lines(1, p, c), hi)))
        o = jnp.dot(jnp.concatenate([ah, al, ah], axis=1), w_op[...], preferred_element_type=F32)
        xr = o[:BLK, :BLK] - o[BLK:, BLK:]
        xi = o[:BLK, BLK:] + o[BLK:, :BLK]
        xhi, xlo = split(lanes(xr, xi))
        if p == 0:
            end = n_blk * BLK
            xh[PAD:2 * PAD, :], xl[PAD:2 * PAD, :] = xhi[:PAD], xlo[:PAD]
            xh[end:end + PAD, :], xl[end:end + PAD, :] = xhi[PAD:], xlo[PAD:]
            pack_first(to_u, xr, xi)
            pack_last(to_d, xr, xi)
        else:
            at = pl.ds(chunk_start(p, c) + PAD, BLK)
            xh[at, :] = xhi
            xl[at, :] = xlo

    if n_src > 2:
        learn(0)
        tell(1)
    receivers(0)
    each([(has_u, lambda: copy_u().start()), (has_d, lambda: copy_d().start())])
    for p in range(HOLD, n_blk):
        send(p)
    for k, op in enumerate(operator_blocks([source_taps(k) for k in range(1, n_blk)]), 1):
        keep_source_operator(k, *op)
    for t in range(2, n_src - 1):
        learn(t - 1)
        tell(t)
    receivers(1)

    def halo_sources():
        each([(has_u, lambda: copy_d().wait_recv()), (has_d, lambda: copy_u().wait_recv())])
        zero = jnp.zeros((8, BLK), F32)
        u8, d8 = from_u[64:72, :], from_d[64:72, :]
        pad = jnp.zeros((24, 2 * BLK), F32)
        top = jnp.concatenate([
            pad,
            lanes(jnp.where(sub, u8, zero), pltpu.roll(jnp.where(sub, zero, u8), 4, 0)),
            lanes(from_u[0:32, :], from_u[32:64, :])], axis=0)
        low = jnp.concatenate([
            lanes(from_d[0:32, :], from_d[32:64, :]),
            lanes(jnp.where(sub, zero, d8), pltpu.roll(jnp.where(sub, d8, zero), 4, 0)),
            pad], axis=0)
        end = PAD + n_blk * BLK
        xh[0:PAD, :], xl[0:PAD, :] = split(top)
        xh[end:end + PAD, :], xl[end:end + PAD, :] = split(low)

    def sources(k):
        b = lax.rem(quarter + k, n_blk)
        r = pl.multiple_of(b * BLK, BLK)
        o = dot3(s_op[b, :, :WIN], s_op[b, :, WIN:], xh[pl.ds(r, WIN), :], xl[pl.ds(r, WIN), :])
        yr = o[:BLK, :BLK] - o[BLK:, BLK:]
        out_ref[0, 0, pl.ds(r, BLK), :] = yr
        out_ref[1, 0, pl.ds(r, BLK), :] = o[:BLK, BLK:] + o[BLK:, :BLK]
        return yr

    n_peer = n_src * n_freq

    def copy_image(d):
        e = lax.rem(h + lax.rem(n_src // 2 + d // n_freq, n_src), n_src)
        return pltpu.make_async_remote_copy(
            img_mine, img_all.at[f], f_send.at[d], f_recv.at[f],
            device_id={"src": e, "freq": lax.rem(f + d, n_freq)}, device_id_type=MESH)

    own = (n_src - n_src // 2) % n_src * n_freq

    def each_peer(act):
        def one(d, _):
            act(copy_image(d))
            return 0
        lax.fori_loop(0, own, one, 0)
        lax.fori_loop(own + 1, n_peer, one, 0)

    def diagonal():
        yr = sources(0)
        pl.when(owner)(lambda: hand_out(yr))

    def hand_out(yr):
        learn(n_src - 2)
        on = lax.broadcasted_iota(jnp.int32, (BLK, BLK), 0) == lax.broadcasted_iota(jnp.int32, (BLK, BLK), 1)
        diag = jnp.sum(jnp.where(on, yr, 0.0), axis=0, keepdims=True)
        img_mine[...] = diag
        img_all[f] = diag
        each_peer(lambda copy: copy.start())

    outer = jnp.logical_or(quarter == 0, quarter == n_blk - 1)
    inner = jnp.logical_not(outer)
    each([(outer, halo_sources), (inner, lambda: receivers(2))])
    diagonal()
    each([(inner, halo_sources), (outer, lambda: receivers(2))])
    receivers(3)
    for k in range(1, n_blk):
        sources(k)

    def got(i, _):
        @pl.when(jnp.logical_not(jnp.logical_and(owner, f == i)))
        def _():
            pltpu.make_async_remote_copy(
                img_mine, img_all.at[i], f_send.at[0], f_recv.at[i],
                device_id={"src": h, "freq": f}, device_id_type=MESH).wait_recv()
        return 0
    pl.when(jnp.logical_not(owner))(lambda: learn(n_src - 2))
    lax.fori_loop(0, n_freq, got, 0)
    total = img_all[0]
    for i in range(1, n_freq):
        total = total + img_all[i]
    img_ref[...] = total

    pl.when(owner)(lambda: each_peer(lambda copy: copy.wait_send()))

    for p in range(n_blk):
        each([(has_l, lambda: copy_l(p).wait_send()), (has_r, lambda: copy_r(p).wait_send())])
    each([(has_u, lambda: copy_u().wait_send()), (has_d, lambda: copy_d().wait_send())])


def body(n_src, n_rcv, n_freq, wavefield, op_table, vel_index, interp_index, interp_weight, freq_perm):
    n_blk = wavefield.shape[2] // BLK
    n_tab, n_vel = op_table.shape[1], interp_index.shape[0]
    vmem = pl.BlockSpec(memory_space=pltpu.VMEM)
    smem = pl.BlockSpec(memory_space=pltpu.SMEM)
    stay = pl.BlockSpec(memory_space=pl.ANY)
    dma, flag = pltpu.SemaphoreType.DMA, pltpu.SemaphoreType.REGULAR
    slabs = [pltpu.VMEM((n_blk, SLAB, BLK), F32)] * 4 + [pltpu.VMEM((SLAB, BLK), F32)] * 4
    length = 2 * PAD + n_blk * BLK
    sunk, image = pl.pallas_call(
        functools.partial(kernel, n_src, n_rcv, n_freq),
        out_shape=(pltpu.VMEM(wavefield.shape, F32), pltpu.VMEM((1, BLK), F32)),
        in_specs=[stay, stay, stay, stay, stay, smem],
        out_specs=(vmem, vmem),
        scratch_shapes=[
            pltpu.VMEM((2, 32, n_tab), F32),
            pltpu.VMEM((BLK, BLK), F32),
            pltpu.VMEM((n_vel, 2 * WIN), F32),
            pltpu.VMEM((WIN, 2 * WIN), F32),
            pltpu.VMEM((length, 2 * WIN), F32),
            pltpu.VMEM((3 * WIN, WIN), BF),
            pltpu.VMEM((n_blk, WIN, 2 * WIN), BF),
            pltpu.VMEM((length, WIN), BF),
            pltpu.VMEM((length, WIN), BF),
            *slabs,
            pltpu.VMEM((1, BLK), F32),
            pltpu.VMEM((n_freq, 1, BLK), F32),
            pltpu.VMEM(wavefield.shape, F32),
            pltpu.VMEM((TAPS, 2, n_tab), F32),
            pltpu.SMEM(vel_index.shape, jnp.int32),
            pltpu.VMEM(interp_index.shape[::-1], jnp.int32),
            pltpu.VMEM(interp_index.shape[::-1], F32),
            dma((10,)),
            dma((2, n_blk)), dma((2, n_blk)), dma((2,)), dma((2,)),
            dma((n_src * n_freq,)), dma((n_freq,)), flag((n_src - 1,)), flag((n_src - 1,)),
        ],
        compiler_params=pltpu.CompilerParams(collective_id=0, has_side_effects=True),
        name="depth_step",
    )(wavefield, jnp.transpose(op_table, (2, 0, 1)), vel_index, interp_index.T, interp_weight.T, freq_perm)
    return sunk, image.reshape(BLK)


def solution(mesh):
    sizes = [mesh.shape[a] for a in ("src", "rcv", "freq")]
    in_specs = (P(None, "freq", "src", "rcv"), P(), P(), P(), P(), P("freq"))
    out_specs = (P(None, "freq", "src", "rcv"), P("rcv"))
    return jax.shard_map(functools.partial(body, *sizes), mesh=mesh, in_specs=in_specs, out_specs=out_specs,
                         check_vma=False)
```

```python
import functools

import jax
import jax.numpy as jnp
from jax import lax
from jax.experimental import pallas as pl
from jax.experimental.pallas import tpu as pltpu
from jax.sharding import PartitionSpec as P

MESH = pl.DeviceIdType.MESH
F32 = jnp.float32
BF = jnp.bfloat16
TILE = 16
TAPS = 19
HALO = 36
BLK = 128
PAD = 64
WIN = 256
HOLD = 3
SLAB = 72


def split(x):
    hi = x.astype(BF)
    return hi, (x - hi.astype(F32)).astype(BF)


def dot3(ah, al, bh, bl):
    a = jnp.concatenate([ah, al, ah], axis=1)
    b = jnp.concatenate([bh, bh, bl], axis=0)
    return jnp.dot(a, b, preferred_element_type=F32)


def rows(a, b):
    return jnp.concatenate([a, b], axis=0)


def lanes(a, b):
    return jnp.concatenate([a, b], axis=1)


def operator_blocks(taps):
    near, mid = slice(PAD // 2, WIN - PAD // 2), slice(PAD, PAD + BLK)

    def parts(re, im):
        return [split(re), split(im), split(re + im)]

    def products(three, at):
        return [dot3(h[at], l[at], h, l) for h, l in three]

    def whole(x):
        edge = jnp.zeros((PAD // 2, WIN), F32)
        return jnp.concatenate([edge, x, edge], axis=0)

    ones = [[pltpu.roll(x, 0, 1, stride=1, stride_axis=0) for x in pair] for pair in taps]
    ones = [parts(*pair) for pair in ones]
    twos = [products(three, near) for three in ones]
    twos = [parts(whole(p - q), whole(r - p - q)) for p, q, r in twos]
    fours = [products(three, mid) for three in twos]
    return [(p - q, r - p - q) for p, q, r in fours]


def upper_half():
    return lax.broadcasted_iota(jnp.int32, (8, BLK), 0) >= 4


def pack_last(buf, xr, xi):
    buf[0:32, :] = xr[96:128]
    buf[32:64, :] = xi[96:128]
    buf[64:72, :] = jnp.where(upper_half(), xr[88:96], pltpu.roll(xi[88:96], 4, 0))


def pack_first(buf, xr, xi):
    buf[0:32, :] = xr[0:32]
    buf[32:64, :] = xi[0:32]
    buf[64:72, :] = jnp.where(upper_half(), pltpu.roll(xi[32:40], 4, 0), xr[32:40])


def kernel(
    n_src, n_rcv, n_freq,
    u_any, op_any, vel_any, idx_any, wgt_any, perm_any,
    out_ref, img_ref,
    raw, turn, mix, crw, cw, w_op, s_op, xh, xl, gh, gl,
    to_l, to_r, from_l, from_r, to_u, to_d, from_u, from_d,
    img_mine, img_all, u_ref, op_ref, vel_ref, idx_ref, wgt_ref, perm_ref,
    in_sem, r_send, r_recv, s_send, s_recv, f_send, f_recv, known_u, known_d,
):
    h = lax.axis_index("src")
    c = lax.axis_index("rcv")
    f = lax.axis_index("freq")
    n_blk = out_ref.shape[2] // BLK
    n_tile = vel_any.shape[0]
    n_tab = op_any.shape[2]
    n_vel = idx_any.shape[1]
    has_l, has_r = c > 0, c < n_rcv - 1
    has_u, has_d = h > 0, h < n_src - 1
    owner = h == c // n_blk
    quarter = lax.rem(c, n_blk)
    first, final = quarter == 0, quarter == n_blk - 1
    helped = jnp.logical_or(jnp.logical_and(first, c // n_blk > 0), jnp.logical_and(final, c // n_blk < n_src - 1))
    helper = jnp.logical_and(helped, h == c // n_blk + jnp.where(first, -1, 1))

    def to(axis, index):
        return dict(device_id={axis: index}, device_id_type=MESH)

    up, down = to("src", jnp.maximum(h - 1, 0)), to("src", jnp.minimum(h + 1, n_src - 1))
    left, right = to("rcv", jnp.maximum(c - 1, 0)), to("rcv", jnp.minimum(c + 1, n_rcv - 1))

    def each(pairs):
        for cond, act in pairs:
            pl.when(cond)(act)

    barrier = pltpu.get_barrier_semaphore()
    each([
        (has_l, lambda: pl.semaphore_signal(barrier, 1, **left)),
        (has_r, lambda: pl.semaphore_signal(barrier, 1, **right)),
        (has_u, lambda: pl.semaphore_signal(barrier, 1, **up)),
        (has_d, lambda: pl.semaphore_signal(barrier, 1, **down)),
    ])
    for d in range(1, n_freq):
        pl.semaphore_signal(barrier, 1, **to("freq", lax.rem(f + d, n_freq)))

    n_row = u_any.shape[2]

    def fetch_lines(part, at, sem):
        return pltpu.make_async_copy(u_any.at[part, 0, at, :], u_ref.at[part, 0, at, :], in_sem.at[sem])

    outer_lines = [
        fetch_lines(part, at, 2 * part + k)
        for part in range(2) for k, at in enumerate([pl.ds(0, PAD), pl.ds(n_row - PAD, PAD)])]
    inner_lines = [fetch_lines(part, pl.ds(PAD, n_row - 2 * PAD), 4 + part) for part in range(2)]
    tables = [
        pltpu.make_async_copy(src, dst, in_sem.at[6 + k])
        for k, (src, dst) in enumerate([(op_any, op_ref), (idx_any, idx_ref), (wgt_any, wgt_ref), (vel_any, vel_ref),
                                     (perm_any, perm_ref)])]
    for copy in outer_lines + tables + inner_lines:
        copy.start()

    n_mid = n_blk - 1

    def chunk_start(p, col):
        back = lax.rem(col, n_blk) >= n_blk // 2
        return pl.multiple_of(PAD + BLK * jnp.where(back, n_mid - p, p - 1), PAD)

    def part_lines(part, p, col):
        if p == 0:
            last = u_ref.shape[2] - PAD
            return rows(u_ref[part, 0, 0:PAD, :], u_ref[part, 0, last:last + PAD, :])
        return u_ref[part, 0, pl.ds(chunk_start(p, col), BLK), :]

    def pack(p):
        pack_first(to_l.at[p], part_lines(0, p, jnp.maximum(c - 1, 0)).T, part_lines(1, p, jnp.maximum(c - 1, 0)).T)
        pack_last(to_r.at[p], part_lines(0, p, c + 1).T, part_lines(1, p, c + 1).T)

    def copy_l(p):
        return pltpu.make_async_remote_copy(to_l.at[p], from_r.at[p], r_send.at[0, p], r_recv.at[0, p], **left)

    def copy_r(p):
        return pltpu.make_async_remote_copy(to_r.at[p], from_l.at[p], r_send.at[1, p], r_recv.at[1, p], **right)

    def copy_u():
        return pltpu.make_async_remote_copy(to_u, from_d, s_send.at[0], s_recv.at[0], **up)

    def copy_d():
        return pltpu.make_async_remote_copy(to_d, from_u, s_send.at[1], s_recv.at[1], **down)

    def send(p):
        each([(has_l, lambda: copy_l(p).start()), (has_r, lambda: copy_r(p).start())])

    def clear(ref):
        ref[...] = jnp.zeros_like(ref)

    each([
        (jnp.logical_not(has_l), lambda: clear(from_l)),
        (jnp.logical_not(has_r), lambda: clear(from_r)),
        (jnp.logical_not(has_u), lambda: clear(from_u)),
        (jnp.logical_not(has_d), lambda: clear(from_d)),
        (jnp.logical_not(helped), lambda: clear(img_all.at[pl.ds(n_freq, n_freq)])),
    ])
    edge = PAD + n_blk * BLK
    for x in (xh, xl):
        clear(x.at[pl.ds(0, PAD)])
        clear(x.at[pl.ds(edge, PAD)])

    for copy in outer_lines:
        copy.wait()
    pack(0)
    ones = lambda cond: cond.astype(jnp.int32)
    pl.semaphore_wait(barrier, ones(has_l) + ones(has_r) + ones(has_u) + ones(has_d) + (n_freq - 1))

    def tell(t):
        each([
            (has_d if t == 0 else jnp.logical_and(has_d, h >= t), lambda: pl.semaphore_signal(known_u.at[t], 1, **down)),
            (has_u if t == 0 else jnp.logical_and(has_u, h <= n_src - 1 - t),
             lambda: pl.semaphore_signal(known_d.at[t], 1, **up)),
        ])

    def learn(t):
        each([
            (h >= t + 1, lambda: pl.semaphore_wait(known_u.at[t], 1)),
            (h <= n_src - 2 - t, lambda: pl.semaphore_wait(known_d.at[t], 1)),
        ])

    tell(0)
    send(0)

    for copy in tables:
        copy.wait()
    clear(raw)
    clear(turn)
    raw[0, 0:TAPS, :] = op_ref[:, 0, :]
    raw[1, 0:TAPS, :] = op_ref[:, 1, :]
    slot = perm_ref[0]
    row = idx_ref[pl.ds(slot, 1), :]
    wgt = wgt_ref[pl.ds(slot, 1), :]
    line = lax.broadcasted_iota(jnp.int32, (n_tab, n_vel), 0)
    table = rows(raw[0], raw[1])
    hi, rest = table.astype(BF), table - table.astype(BF).astype(F32)
    mid, low = split(rest)
    table = jnp.concatenate([hi, mid, low], axis=1)

    def picked(which):
        one = (line == which).astype(F32).astype(BF)
        return jnp.dot(table, jnp.concatenate([one, one, one], axis=0), preferred_element_type=F32)

    turn[0:64, 0:n_vel] = picked(row) * (1.0 - wgt) + picked(row + 1) * wgt
    turned = turn[...].T[0:n_vel]
    few = lax.broadcasted_iota(jnp.int32, (n_vel, BLK), 1) < 32
    none = jnp.zeros((n_vel, BLK), F32)
    for p in range(2):
        part = jnp.where(few, pltpu.roll(turned, (BLK - 32 * p) % BLK, 1), 0.0)
        mix[:, WIN * p:WIN * (p + 1)] = pltpu.roll(lanes(part, none), WIN - TAPS // 2, 1)

    def taps_at(dst, first_tile):
        def one(t, _):
            g = first_tile + t
            inside = jnp.logical_and(g >= 0, g < n_tile).astype(F32)
            v = vel_ref[jnp.clip(g, 0, n_tile - 1)]
            line = mix[pl.ds(v, 1), :] * inside
            dst[pl.ds(pl.multiple_of(t * TILE, TILE), TILE), :] = jnp.broadcast_to(line, (TILE, 2 * WIN))
            return 0
        lax.fori_loop(0, dst.shape[0] // TILE, one, 0)

    for copy in inner_lines:
        copy.wait()
    pack(1)
    send(1)
    for p in range(2, n_blk):
        pack(p)

    sub = upper_half()
    taps_at(crw, (c * BLK - PAD) // TILE)
    taps_at(cw, (h * n_blk * BLK - PAD) // TILE)

    def source_taps(k):
        r = pl.multiple_of(lax.rem(quarter + k, n_blk) * BLK, BLK)
        return cw[pl.ds(r, WIN), :WIN], cw[pl.ds(r, WIN), WIN:]

    def keep_source_operator(k, sr, si):
        b = lax.rem(quarter + k, n_blk)
        sh, sl = split(rows(sr, si))
        s_op[b, :, :WIN] = sh
        s_op[b, :, WIN:] = sl

    (mr, mi), nearest = operator_blocks([(crw[:, :WIN], crw[:, WIN:]), source_taps(0)])
    keep_source_operator(0, *nearest)
    pieces = []
    for m in (mr, mi):
        t = rows(m[:, :BLK].T, m[:, BLK:].T)
        pieces.append(jnp.concatenate([
            t[PAD:PAD + BLK], t[32:64], t[192:224], jnp.where(sub, t[24:32], t[224:232]),
            jnp.zeros((BLK - SLAB, BLK), F32)], axis=0))
    wh, wl = split(lanes(pieces[0], pieces[1]))
    w_op[0:WIN, :] = wh
    w_op[WIN:2 * WIN, :] = wh
    w_op[2 * WIN:, :] = wl

    def receivers(p):
        each([(has_r, lambda: copy_l(p).wait_recv()), (has_l, lambda: copy_r(p).wait_recv())])
        l8, r8 = from_l[p, 64:72, :], from_r[p, 64:72, :]
        zero = jnp.zeros((BLK - SLAB, BLK), F32)
        hr = jnp.concatenate([from_l[p, 0:32, :], from_r[p, 0:32, :], jnp.where(sub, l8, r8), zero], axis=0).T
        hi = jnp.concatenate([from_l[p, 32:64, :], from_r[p, 32:64, :],
                              pltpu.roll(jnp.where(sub, r8, l8), 4, 0), zero], axis=0).T
        ah, al = split(rows(lanes(part_lines(0, p, c), hr), lanes(part_lines(1, p, c), hi)))
        o = jnp.dot(jnp.concatenate([ah, al, ah], axis=1), w_op[...], preferred_element_type=F32)
        xr = o[:BLK, :BLK] - o[BLK:, BLK:]
        xi = o[:BLK, BLK:] + o[BLK:, :BLK]
        xhi, xlo = split(lanes(xr, xi))
        if p == 0:
            end = n_blk * BLK
            xh[PAD:2 * PAD, :], xl[PAD:2 * PAD, :] = xhi[:PAD], xlo[:PAD]
            xh[end:end + PAD, :], xl[end:end + PAD, :] = xhi[PAD:], xlo[PAD:]
            pack_first(to_u, xr, xi)
            pack_last(to_d, xr, xi)
        else:
            at = pl.ds(chunk_start(p, c) + PAD, BLK)
            xh[at, :] = xhi
            xl[at, :] = xlo

    if n_src > 2:
        learn(0)
        tell(1)
    for p in range(2, HOLD):
        send(p)
    receivers(0)
    each([(has_u, lambda: copy_u().start()), (has_d, lambda: copy_d().start())])
    for p in range(HOLD, n_blk):
        send(p)
    def halo_sources():
        each([(has_u, lambda: copy_d().wait_recv()), (has_d, lambda: copy_u().wait_recv())])
        zero = jnp.zeros((8, BLK), F32)
        u8, d8 = from_u[64:72, :], from_d[64:72, :]
        pad = jnp.zeros((24, 2 * BLK), F32)
        top = jnp.concatenate([
            pad,
            lanes(jnp.where(sub, u8, zero), pltpu.roll(jnp.where(sub, zero, u8), 4, 0)),
            lanes(from_u[0:32, :], from_u[32:64, :])], axis=0)
        low = jnp.concatenate([
            lanes(from_d[0:32, :], from_d[32:64, :]),
            lanes(jnp.where(sub, zero, d8), pltpu.roll(jnp.where(sub, d8, zero), 4, 0)),
            pad], axis=0)
        end = PAD + n_blk * BLK
        xh[0:PAD, :], xl[0:PAD, :] = split(top)
        xh[end:end + PAD, :], xl[end:end + PAD, :] = split(low)

    def source_block(k):
        b = lax.rem(quarter + k, n_blk)
        r = pl.multiple_of(b * BLK, BLK)
        o = dot3(s_op[b, :, :WIN], s_op[b, :, WIN:], xh[pl.ds(r, WIN), :], xl[pl.ds(r, WIN), :])
        return r, o

    def sources(k):
        r, o = source_block(k)
        out_ref[0, 0, pl.ds(r, BLK), :] = o[:BLK, :BLK] - o[BLK:, BLK:]
        out_ref[1, 0, pl.ds(r, BLK), :] = o[:BLK, BLK:] + o[BLK:, :BLK]

    n_peer = n_src * n_freq
    mine = f + jnp.where(helper, n_freq, 0)

    def copy_image(d):
        e = lax.rem(h + lax.rem(n_src // 2 + d // n_freq, n_src), n_src)
        return pltpu.make_async_remote_copy(
            img_mine, img_all.at[mine], f_send.at[d], f_recv.at[mine],
            device_id={"src": e, "freq": lax.rem(f + d, n_freq)}, device_id_type=MESH)

    own = (n_src - n_src // 2) % n_src * n_freq

    def each_peer(act):
        def one(d, _):
            act(copy_image(d))
            return 0
        lax.fori_loop(0, own, one, 0)
        lax.fori_loop(own + 1, n_peer, one, 0)

    def keep_diagonal(o):
        on = lax.broadcasted_iota(jnp.int32, (BLK, BLK), 0) == lax.broadcasted_iota(jnp.int32, (BLK, BLK), 1)
        block = o[:BLK, :BLK] - o[BLK:, BLK:]
        diag = jnp.sum(jnp.where(on, block, 0.0), axis=0, keepdims=True)
        img_mine[...] = diag
        img_all[mine] = diag

    def hand_out():
        learn(n_src - 2)
        each_peer(lambda copy: copy.start())

    def diagonal():
        keep_diagonal(source_block(0)[1])
        hand_out()

    def help_diagonal():
        b = jnp.where(first, n_blk, -1)
        taps_at(crw, ((h * n_blk + b) * BLK - PAD) // TILE)
        sr, si = operator_blocks([(crw[:, :WIN], crw[:, WIN:])])[0]
        sh, sl = split(rows(sr, si))
        clear(gh)
        clear(gl)
        at = pl.ds(pl.multiple_of(jnp.where(first, 0, WIN - PAD), PAD), PAD)
        own = pl.ds(pl.multiple_of(jnp.where(first, edge - PAD, PAD), PAD), PAD)
        gh[at, :] = xh[own, :]
        gl[at, :] = xl[own, :]
        keep_diagonal(dot3(sh, sl, gh[...], gl[...]))

    pl.when(helper)(help_diagonal)
    for t in range(2, n_src - 1):
        learn(t - 1)
        tell(t)
    pl.when(helper)(hand_out)
    receivers(1)
    outer = jnp.logical_or(first, final)
    pl.when(jnp.logical_and(owner, outer))(diagonal)
    for k, op in enumerate(operator_blocks([source_taps(k) for k in range(1, n_blk)]), 1):
        keep_source_operator(k, *op)
    receivers(2)
    pl.when(jnp.logical_and(owner, jnp.logical_not(outer)))(diagonal)
    halo_sources()
    receivers(3)
    for k in range(n_blk):
        sources(k)

    def got(i, _):
        sender, there = jnp.where(i < n_freq, owner, helper), jnp.where(i < n_freq, True, helped)

        @pl.when(jnp.logical_and(there, jnp.logical_not(jnp.logical_and(sender, f == lax.rem(i, n_freq)))))
        def _():
            pltpu.make_async_remote_copy(
                img_mine, img_all.at[i], f_send.at[0], f_recv.at[i],
                device_id={"src": h, "freq": f}, device_id_type=MESH).wait_recv()
        return 0
    giver = jnp.logical_or(owner, helper)
    pl.when(giver)(lambda: each_peer(lambda copy: copy.wait_send()))

    for p in range(n_blk):
        each([(has_l, lambda: copy_l(p).wait_send()), (has_r, lambda: copy_r(p).wait_send())])
    each([(has_u, lambda: copy_u().wait_send()), (has_d, lambda: copy_d().wait_send())])
    pl.when(jnp.logical_not(giver))(lambda: learn(n_src - 2))
    lax.fori_loop(0, 2 * n_freq, got, 0)
    total = img_all[0]
    for i in range(1, 2 * n_freq):
        total = total + img_all[i]
    img_ref[...] = total


def body(n_src, n_rcv, n_freq, wavefield, op_table, vel_index, interp_index, interp_weight, freq_perm):
    n_blk = wavefield.shape[2] // BLK
    n_tab, n_vel = op_table.shape[1], interp_index.shape[0]
    vmem = pl.BlockSpec(memory_space=pltpu.VMEM)
    stay = pl.BlockSpec(memory_space=pl.ANY)
    dma, flag = pltpu.SemaphoreType.DMA, pltpu.SemaphoreType.REGULAR
    slabs = [pltpu.VMEM((n_blk, SLAB, BLK), F32)] * 4 + [pltpu.VMEM((SLAB, BLK), F32)] * 4
    length = 2 * PAD + n_blk * BLK
    sunk, image = pl.pallas_call(
        functools.partial(kernel, n_src, n_rcv, n_freq),
        out_shape=(pltpu.VMEM(wavefield.shape, F32), pltpu.VMEM((1, BLK), F32)),
        in_specs=[stay] * 6,
        out_specs=(vmem, vmem),
        scratch_shapes=[
            pltpu.VMEM((2, 32, n_tab), F32),
            pltpu.VMEM((BLK, BLK), F32),
            pltpu.VMEM((n_vel, 2 * WIN), F32),
            pltpu.VMEM((WIN, 2 * WIN), F32),
            pltpu.VMEM((length, 2 * WIN), F32),
            pltpu.VMEM((3 * WIN, WIN), BF),
            pltpu.VMEM((n_blk, WIN, 2 * WIN), BF),
            pltpu.VMEM((length, WIN), BF),
            pltpu.VMEM((length, WIN), BF),
            pltpu.VMEM((WIN, WIN), BF),
            pltpu.VMEM((WIN, WIN), BF),
            *slabs,
            pltpu.VMEM((1, BLK), F32),
            pltpu.VMEM((2 * n_freq, 1, BLK), F32),
            pltpu.VMEM(wavefield.shape, F32),
            pltpu.VMEM((TAPS, 2, n_tab), F32),
            pltpu.SMEM(vel_index.shape, jnp.int32),
            pltpu.VMEM(interp_index.shape[::-1], jnp.int32),
            pltpu.VMEM(interp_index.shape[::-1], F32),
            pltpu.SMEM(freq_perm.shape, jnp.int32),
            dma((11,)),
            dma((2, n_blk)), dma((2, n_blk)), dma((2,)), dma((2,)),
            dma((n_src * n_freq,)), dma((2 * n_freq,)), flag((n_src - 1,)), flag((n_src - 1,)),
        ],
        compiler_params=pltpu.CompilerParams(collective_id=0, has_side_effects=True),
        name="depth_step",
    )(wavefield, jnp.transpose(op_table, (2, 0, 1)), vel_index, interp_index.T, interp_weight.T, freq_perm)
    return sunk, image.reshape(BLK)


def solution(mesh):
    sizes = [mesh.shape[a] for a in ("src", "rcv", "freq")]
    in_specs = (P(None, "freq", "src", "rcv"), P(), P(), P(), P(), P("freq"))
    out_specs = (P(None, "freq", "src", "rcv"), P("rcv"))
    return jax.shard_map(functools.partial(body, *sizes), mesh=mesh, in_specs=in_specs, out_specs=out_specs,
                         check_vma=False)
```

```python
import functools

import jax
import jax.numpy as jnp
from jax import lax
from jax.experimental import pallas as pl
from jax.experimental.pallas import tpu as pltpu
from jax.sharding import PartitionSpec as P

MESH = pl.DeviceIdType.MESH
F32 = jnp.float32
BF = jnp.bfloat16
TILE = 16
TAPS = 19
HALO = 36
BLK = 128
PAD = 64
WIN = 256
HOLD = 3
SLAB = 72


def split(x):
    hi = x.astype(BF)
    return hi, (x - hi.astype(F32)).astype(BF)


def dot3(ah, al, bh, bl):
    a = jnp.concatenate([ah, al, ah], axis=1)
    b = jnp.concatenate([bh, bh, bl], axis=0)
    return jnp.dot(a, b, preferred_element_type=F32)


def rows(a, b):
    return jnp.concatenate([a, b], axis=0)


def lanes(a, b):
    return jnp.concatenate([a, b], axis=1)


def operator_blocks(taps):
    near, mid = slice(PAD // 2, WIN - PAD // 2), slice(PAD, PAD + BLK)

    def parts(re, im):
        return [split(re), split(im), split(re + im)]

    def products(three, at):
        return [dot3(h[at], l[at], h, l) for h, l in three]

    def whole(x):
        edge = jnp.zeros((PAD // 2, WIN), F32)
        return jnp.concatenate([edge, x, edge], axis=0)

    ones = [[pltpu.roll(x, 0, 1, stride=1, stride_axis=0) for x in pair] for pair in taps]
    ones = [parts(*pair) for pair in ones]
    twos = [products(three, near) for three in ones]
    twos = [parts(whole(p - q), whole(r - p - q)) for p, q, r in twos]
    fours = [products(three, mid) for three in twos]
    return [(p - q, r - p - q) for p, q, r in fours]


def upper_half():
    return lax.broadcasted_iota(jnp.int32, (8, BLK), 0) >= 4


def pack_last(buf, xr, xi):
    buf[0:32, :] = xr[96:128]
    buf[32:64, :] = xi[96:128]
    buf[64:72, :] = jnp.where(upper_half(), xr[88:96], pltpu.roll(xi[88:96], 4, 0))


def pack_first(buf, xr, xi):
    buf[0:32, :] = xr[0:32]
    buf[32:64, :] = xi[0:32]
    buf[64:72, :] = jnp.where(upper_half(), pltpu.roll(xi[32:40], 4, 0), xr[32:40])


def kernel(
    n_src, n_rcv, n_freq,
    u_any, op_any, vel_any, idx_any, wgt_any, perm_any,
    out_ref, img_ref,
    raw, turn, mix, crw, cw, w_op, s_op, h_op, xh, xl, gh, gl,
    to_l, to_r, from_l, from_r, to_u, to_d, from_u, from_d,
    img_mine, img_all, img_out, u_ref, op_ref, vel_ref, idx_ref, wgt_ref, perm_ref,
    in_sem, r_send, r_recv, s_send, s_recv, f_send, f_recv, known_u, known_d,
):
    h = lax.axis_index("src")
    c = lax.axis_index("rcv")
    f = lax.axis_index("freq")
    n_blk = out_ref.shape[2] // BLK
    n_tile = vel_any.shape[0]
    n_tab = op_any.shape[2]
    n_vel = idx_any.shape[1]
    has_l, has_r = c > 0, c < n_rcv - 1
    has_u, has_d = h > 0, h < n_src - 1
    owner = h == c // n_blk
    quarter = lax.rem(c, n_blk)
    first, final = quarter == 0, quarter == n_blk - 1
    helped = jnp.logical_or(jnp.logical_and(first, c // n_blk > 0), jnp.logical_and(final, c // n_blk < n_src - 1))
    helper = jnp.logical_and(helped, h == c // n_blk + jnp.where(first, -1, 1))

    def to(axis, index):
        return dict(device_id={axis: index}, device_id_type=MESH)

    up, down = to("src", jnp.maximum(h - 1, 0)), to("src", jnp.minimum(h + 1, n_src - 1))
    left, right = to("rcv", jnp.maximum(c - 1, 0)), to("rcv", jnp.minimum(c + 1, n_rcv - 1))

    def each(pairs):
        for cond, act in pairs:
            pl.when(cond)(act)

    n_row = u_any.shape[2]

    def fetch_lines(start, size, sem):
        at = pl.ds(start, size)
        return pltpu.make_async_copy(u_any.at[:, 0, at, :], u_ref.at[:, 0, at, :], in_sem.at[sem])

    outer_lines = [fetch_lines(0, PAD, 0), fetch_lines(n_row - PAD, PAD, 1)]
    for copy in outer_lines:
        copy.start()

    barrier = pltpu.get_barrier_semaphore()
    each([
        (has_l, lambda: pl.semaphore_signal(barrier, 1, **left)),
        (has_r, lambda: pl.semaphore_signal(barrier, 1, **right)),
        (has_u, lambda: pl.semaphore_signal(barrier, 1, **up)),
        (has_d, lambda: pl.semaphore_signal(barrier, 1, **down)),
    ])
    for d in range(1, n_freq):
        pl.semaphore_signal(barrier, 1, **to("freq", lax.rem(f + d, n_freq)))

    inner_lines = [fetch_lines(PAD, n_row - 2 * PAD, 2)]
    tables = [
        pltpu.make_async_copy(src, dst, in_sem.at[3 + k])
        for k, (src, dst) in enumerate([(op_any, op_ref), (idx_any, idx_ref), (wgt_any, wgt_ref), (vel_any, vel_ref),
                                     (perm_any, perm_ref)])]
    for copy in tables + inner_lines:
        copy.start()

    n_mid = n_blk - 1

    def chunk_start(p, col):
        back = lax.rem(col, n_blk) >= n_blk // 2
        return pl.multiple_of(PAD + BLK * jnp.where(back, n_mid - p, p - 1), PAD)

    def part_lines(part, p, col):
        if p == 0:
            last = u_ref.shape[2] - PAD
            return rows(u_ref[part, 0, 0:PAD, :], u_ref[part, 0, last:last + PAD, :])
        return u_ref[part, 0, pl.ds(chunk_start(p, col), BLK), :]

    def pack(p):
        if p == 0:
            tr, ti = part_lines(0, 0, c).T, part_lines(1, 0, c).T
            pack_first(to_l.at[0], tr, ti)
            pack_last(to_r.at[0], tr, ti)
            return
        pack_first(to_l.at[p], part_lines(0, p, jnp.maximum(c - 1, 0)).T, part_lines(1, p, jnp.maximum(c - 1, 0)).T)
        pack_last(to_r.at[p], part_lines(0, p, c + 1).T, part_lines(1, p, c + 1).T)

    def copy_l(p):
        return pltpu.make_async_remote_copy(to_l.at[p], from_r.at[p], r_send.at[0], r_recv.at[0, p], **left)

    def copy_r(p):
        return pltpu.make_async_remote_copy(to_r.at[p], from_l.at[p], r_send.at[1], r_recv.at[1, p], **right)

    def copy_u():
        return pltpu.make_async_remote_copy(to_u, from_d, s_send.at[0], s_recv.at[0], **up)

    def copy_d():
        return pltpu.make_async_remote_copy(to_d, from_u, s_send.at[1], s_recv.at[1], **down)

    def send(p):
        each([(has_l, lambda: copy_l(p).start()), (has_r, lambda: copy_r(p).start())])

    def clear(ref):
        ref[...] = jnp.zeros_like(ref)

    each([
        (jnp.logical_not(has_l), lambda: clear(from_l)),
        (jnp.logical_not(has_r), lambda: clear(from_r)),
        (jnp.logical_not(has_u), lambda: clear(from_u)),
        (jnp.logical_not(has_d), lambda: clear(from_d)),
    ])

    for copy in outer_lines:
        copy.wait()
    pack(0)
    ones = lambda cond: cond.astype(jnp.int32)
    pl.semaphore_wait(barrier, ones(has_l) + ones(has_r) + ones(has_u) + ones(has_d) + (n_freq - 1))

    def tell(t):
        each([
            (has_d if t == 0 else jnp.logical_and(has_d, h >= t), lambda: pl.semaphore_signal(known_u.at[t], 1, **down)),
            (has_u if t == 0 else jnp.logical_and(has_u, h <= n_src - 1 - t),
             lambda: pl.semaphore_signal(known_d.at[t], 1, **up)),
        ])

    def learn(t):
        each([
            (h >= t + 1, lambda: pl.semaphore_wait(known_u.at[t], 1)),
            (h <= n_src - 2 - t, lambda: pl.semaphore_wait(known_d.at[t], 1)),
        ])

    tell(0)
    send(0)

    edge = PAD + n_blk * BLK
    for x in (xh, xl):
        clear(x.at[pl.ds(0, PAD)])
        clear(x.at[pl.ds(edge, PAD)])
    pl.when(jnp.logical_not(helped))(lambda: clear(img_all.at[pl.ds(n_freq, n_freq)]))
    for copy in tables:
        copy.wait()
    clear(raw)
    clear(turn)
    raw[0, 0:TAPS, :] = op_ref[:, 0, :]
    raw[1, 0:TAPS, :] = op_ref[:, 1, :]
    slot = perm_ref[0]
    row = idx_ref[pl.ds(slot, 1), :]
    wgt = wgt_ref[pl.ds(slot, 1), :]
    line = lax.broadcasted_iota(jnp.int32, (n_tab, n_vel), 0)
    table = rows(raw[0], raw[1])
    hi, rest = table.astype(BF), table - table.astype(BF).astype(F32)
    mid, low = split(rest)
    table = jnp.concatenate([hi, mid, low], axis=1)

    def picked(which):
        one = (line == which).astype(F32).astype(BF)
        return jnp.dot(table, jnp.concatenate([one, one, one], axis=0), preferred_element_type=F32)

    turn[0:64, 0:n_vel] = picked(row) * (1.0 - wgt) + picked(row + 1) * wgt
    turned = turn[...].T[0:n_vel]
    few = lax.broadcasted_iota(jnp.int32, (n_vel, BLK), 1) < 32
    none = jnp.zeros((n_vel, BLK), F32)
    for p in range(2):
        part = jnp.where(few, pltpu.roll(turned, (BLK - 32 * p) % BLK, 1), 0.0)
        mix[:, WIN * p:WIN * (p + 1)] = pltpu.roll(lanes(part, none), WIN - TAPS // 2, 1)

    def taps_at(dst, first_tile):
        def one(t, _):
            g = first_tile + t
            inside = jnp.logical_and(g >= 0, g < n_tile).astype(F32)
            v = vel_ref[jnp.clip(g, 0, n_tile - 1)]
            line = mix[pl.ds(v, 1), :] * inside
            dst[pl.ds(pl.multiple_of(t * TILE, TILE), TILE), :] = jnp.broadcast_to(line, (TILE, 2 * WIN))
            return 0
        lax.fori_loop(0, dst.shape[0] // TILE, one, 0)

    for copy in inner_lines:
        copy.wait()
    pack(1)
    send(1)
    for p in range(2, n_blk):
        pack(p)

    sub = upper_half()
    taps_at(crw, (c * BLK - PAD) // TILE)
    taps_at(cw, (h * n_blk * BLK - PAD) // TILE)

    def source_taps(k):
        r = pl.multiple_of(lax.rem(quarter + k, n_blk) * BLK, BLK)
        return cw[pl.ds(r, WIN), :WIN], cw[pl.ds(r, WIN), WIN:]

    def keep_source_operator(k, sr, si):
        b = lax.rem(quarter + k, n_blk)
        sh, sl = split(rows(sr, si))
        s_op[b, :, :WIN] = sh
        s_op[b, :, WIN:] = sl

    (mr, mi), nearest = operator_blocks([(crw[:, :WIN], crw[:, WIN:]), source_taps(0)])
    keep_source_operator(0, *nearest)
    pieces = []
    for m in (mr, mi):
        t = rows(m[:, :BLK].T, m[:, BLK:].T)
        pieces.append(jnp.concatenate([
            t[PAD:PAD + BLK], t[32:64], t[192:224], jnp.where(sub, t[24:32], t[224:232]),
            jnp.zeros((BLK - SLAB, BLK), F32)], axis=0))
    wh, wl = split(lanes(pieces[0], pieces[1]))
    w_op[0:WIN, :] = wh
    w_op[WIN:2 * WIN, :] = wh
    w_op[2 * WIN:, :] = wl

    def receivers(p):
        each([(has_r, lambda: copy_l(p).wait_recv()), (has_l, lambda: copy_r(p).wait_recv())])
        l8, r8 = from_l[p, 64:72, :], from_r[p, 64:72, :]
        zero = jnp.zeros((BLK - SLAB, BLK), F32)
        hr = jnp.concatenate([from_l[p, 0:32, :], from_r[p, 0:32, :], jnp.where(sub, l8, r8), zero], axis=0).T
        hi = jnp.concatenate([from_l[p, 32:64, :], from_r[p, 32:64, :],
                              pltpu.roll(jnp.where(sub, r8, l8), 4, 0), zero], axis=0).T
        ah, al = split(rows(lanes(part_lines(0, p, c), hr), lanes(part_lines(1, p, c), hi)))
        o = jnp.dot(jnp.concatenate([ah, al, ah], axis=1), w_op[...], preferred_element_type=F32)
        xr = o[:BLK, :BLK] - o[BLK:, BLK:]
        xi = o[:BLK, BLK:] + o[BLK:, :BLK]
        xhi, xlo = split(lanes(xr, xi))
        if p == 0:
            end = n_blk * BLK
            xh[PAD:2 * PAD, :], xl[PAD:2 * PAD, :] = xhi[:PAD], xlo[:PAD]
            xh[end:end + PAD, :], xl[end:end + PAD, :] = xhi[PAD:], xlo[PAD:]
            pack_first(to_u, xr, xi)
            pack_last(to_d, xr, xi)
        else:
            at = pl.ds(chunk_start(p, c) + PAD, BLK)
            xh[at, :] = xhi
            xl[at, :] = xlo

    if n_src > 2:
        learn(0)
        tell(1)
    for p in range(2, HOLD):
        send(p)

    def make_helper_operator():
        b = jnp.where(first, n_blk, -1)
        taps_at(crw, ((h * n_blk + b) * BLK - PAD) // TILE)
        sr, si = operator_blocks([(crw[:, :WIN], crw[:, WIN:])])[0]
        sh, sl = split(rows(sr, si))
        h_op[:, :WIN] = sh
        h_op[:, WIN:] = sl

    pl.when(helper)(make_helper_operator)
    receivers(0)
    each([(has_u, lambda: copy_u().start()), (has_d, lambda: copy_d().start())])
    for p in range(HOLD, n_blk):
        send(p)
    def halo_sources():
        each([(has_u, lambda: copy_d().wait_recv()), (has_d, lambda: copy_u().wait_recv())])
        zero = jnp.zeros((8, BLK), F32)
        u8, d8 = from_u[64:72, :], from_d[64:72, :]
        pad = jnp.zeros((24, 2 * BLK), F32)
        top = jnp.concatenate([
            pad,
            lanes(jnp.where(sub, u8, zero), pltpu.roll(jnp.where(sub, zero, u8), 4, 0)),
            lanes(from_u[0:32, :], from_u[32:64, :])], axis=0)
        low = jnp.concatenate([
            lanes(from_d[0:32, :], from_d[32:64, :]),
            lanes(jnp.where(sub, zero, d8), pltpu.roll(jnp.where(sub, d8, zero), 4, 0)),
            pad], axis=0)
        end = PAD + n_blk * BLK
        xh[0:PAD, :], xl[0:PAD, :] = split(top)
        xh[end:end + PAD, :], xl[end:end + PAD, :] = split(low)

    def source_block(k):
        b = lax.rem(quarter + k, n_blk)
        r = pl.multiple_of(b * BLK, BLK)
        o = dot3(s_op[b, :, :WIN], s_op[b, :, WIN:], xh[pl.ds(r, WIN), :], xl[pl.ds(r, WIN), :])
        return r, o

    def sources(k):
        r, o = source_block(k)
        out_ref[0, 0, pl.ds(r, BLK), :] = o[:BLK, :BLK] - o[BLK:, BLK:]
        out_ref[1, 0, pl.ds(r, BLK), :] = o[:BLK, BLK:] + o[BLK:, :BLK]

    mine = f + jnp.where(helper, n_freq, 0)

    near = jnp.where(h == n_src - 1, n_src - 1, 1)
    groups = [n_src // 2, near, 0, n_src - near] if n_src == 4 else [*range(1, n_src), 0]

    def each_peer(group, act):
        def one(d, _):
            act(pltpu.make_async_remote_copy(
                img_mine, img_all.at[mine], f_send, f_recv.at[jnp.where(helper, 1, 0)],
                device_id={"src": lax.rem(h + groups[group], n_src), "freq": lax.rem(f + d, n_freq)},
                device_id_type=MESH))
            return 0
        own = isinstance(groups[group], int) and groups[group] == 0
        lax.fori_loop(int(own), n_freq, one, 0)

    def keep_diagonal(o):
        on = lax.broadcasted_iota(jnp.int32, (BLK, BLK), 0) == lax.broadcasted_iota(jnp.int32, (BLK, BLK), 1)
        block = o[:BLK, :BLK] - o[BLK:, BLK:]
        diag = jnp.sum(jnp.where(on, block, 0.0), axis=0, keepdims=True)
        img_mine[...] = diag
        img_all[mine] = diag

    def hand_out():
        for group in range(n_src - 1):
            each_peer(group, lambda copy: copy.start())

    def hand_last():
        learn(n_src - 2)
        each_peer(n_src - 1, lambda copy: copy.start())

    def diagonal():
        keep_diagonal(source_block(0)[1])
        hand_out()

    def help_diagonal():
        clear(gh)
        clear(gl)
        at = pl.ds(pl.multiple_of(jnp.where(first, 0, WIN - PAD), PAD), PAD)
        own = pl.ds(pl.multiple_of(jnp.where(first, edge - PAD, PAD), PAD), PAD)
        gh[at, :] = xh[own, :]
        gl[at, :] = xl[own, :]
        keep_diagonal(dot3(h_op[:, :WIN], h_op[:, WIN:], gh[...], gl[...]))

    pl.when(helper)(help_diagonal)
    for t in range(2, n_src - 1):
        learn(t - 1)
        tell(t)
    pl.when(helper)(hand_out)
    receivers(1)
    outer = jnp.logical_or(first, final)
    pl.when(jnp.logical_and(owner, outer))(diagonal)
    for k, op in enumerate(operator_blocks([source_taps(k) for k in range(1, n_blk)]), 1):
        keep_source_operator(k, *op)
    giver = jnp.logical_or(owner, helper)
    inner = jnp.logical_and(owner, jnp.logical_not(outer))
    pl.when(jnp.logical_and(giver, jnp.logical_not(inner)))(hand_last)
    receivers(2)
    pl.when(inner)(diagonal)
    pl.when(inner)(hand_last)
    halo_sources()
    receivers(3)
    for k in range(n_blk):
        sources(k)

    def line_copy(size, sem):
        at = pl.ds(0, size)
        return pltpu.make_async_remote_copy(
            img_out.at[at], img_out.at[at], f_send, f_recv.at[sem],
            device_id={"src": h, "freq": f}, device_id_type=MESH)

    all_l = pltpu.make_async_remote_copy(to_l, from_r, r_send.at[0], r_recv.at[0, 0], **left)
    all_r = pltpu.make_async_remote_copy(to_r, from_l, r_send.at[1], r_recv.at[1, 0], **right)
    each([
        (giver, lambda: line_copy(n_src * n_freq - 1, 0).wait_send()),
        (has_l, all_l.wait_send),
        (has_r, all_r.wait_send),
        (has_u, lambda: copy_u().wait_send()),
        (has_d, lambda: copy_d().wait_send()),
        (jnp.logical_not(giver), lambda: learn(n_src - 2)),
    ])
    not_mine = n_freq - 1

    def got():
        others, helpers = jnp.logical_not(owner), jnp.logical_and(helped, jnp.logical_not(helper))
        each([
            (others, lambda: line_copy(n_freq, 0).wait_recv()),
            (helpers, lambda: line_copy(n_freq, 1).wait_recv()),
        ])
        if not_mine:
            each([
                (owner, lambda: line_copy(not_mine, 0).wait_recv()),
                (helper, lambda: line_copy(not_mine, 1).wait_recv()),
            ])

    got()
    total = img_all[0]
    for i in range(1, 2 * n_freq):
        total = total + img_all[i]
    img_ref[...] = total


def body(n_src, n_rcv, n_freq, wavefield, op_table, vel_index, interp_index, interp_weight, freq_perm):
    n_blk = wavefield.shape[2] // BLK
    n_tab, n_vel = op_table.shape[1], interp_index.shape[0]
    vmem = pl.BlockSpec(memory_space=pltpu.VMEM)
    stay = pl.BlockSpec(memory_space=pl.ANY)
    dma, flag = pltpu.SemaphoreType.DMA, pltpu.SemaphoreType.REGULAR
    slabs = [pltpu.VMEM((n_blk, SLAB, BLK), F32)] * 4 + [pltpu.VMEM((SLAB, BLK), F32)] * 4
    length = 2 * PAD + n_blk * BLK
    sunk, image = pl.pallas_call(
        functools.partial(kernel, n_src, n_rcv, n_freq),
        out_shape=(pltpu.VMEM(wavefield.shape, F32), pltpu.VMEM((1, BLK), F32)),
        in_specs=[stay] * 6,
        out_specs=(vmem, vmem),
        scratch_shapes=[
            pltpu.VMEM((2, 32, n_tab), F32),
            pltpu.VMEM((BLK, BLK), F32),
            pltpu.VMEM((n_vel, 2 * WIN), F32),
            pltpu.VMEM((WIN, 2 * WIN), F32),
            pltpu.VMEM((length, 2 * WIN), F32),
            pltpu.VMEM((3 * WIN, WIN), BF),
            pltpu.VMEM((n_blk, WIN, 2 * WIN), BF),
            pltpu.VMEM((WIN, 2 * WIN), BF),
            pltpu.VMEM((length, WIN), BF),
            pltpu.VMEM((length, WIN), BF),
            pltpu.VMEM((WIN, WIN), BF),
            pltpu.VMEM((WIN, WIN), BF),
            *slabs,
            pltpu.VMEM((1, BLK), F32),
            pltpu.VMEM((2 * n_freq, 1, BLK), F32),
            pltpu.VMEM((n_src * n_freq, 1, BLK), F32),
            pltpu.VMEM(wavefield.shape, F32),
            pltpu.VMEM((TAPS, 2, n_tab), F32),
            pltpu.SMEM(vel_index.shape, jnp.int32),
            pltpu.VMEM(interp_index.shape[::-1], jnp.int32),
            pltpu.VMEM(interp_index.shape[::-1], F32),
            pltpu.SMEM(freq_perm.shape, jnp.int32),
            dma((8,)),
            dma((2,)), dma((2, n_blk)), dma((2,)), dma((2,)),
            dma, dma((2,)), flag((n_src - 1,)), flag((n_src - 1,)),
        ],
        compiler_params=pltpu.CompilerParams(collective_id=0, has_side_effects=True),
        name="depth_step",
    )(wavefield, jnp.transpose(op_table, (2, 0, 1)), vel_index, interp_index.T, interp_weight.T, freq_perm)
    return sunk, image.reshape(BLK)


def solution(mesh):
    sizes = [mesh.shape[a] for a in ("src", "rcv", "freq")]
    in_specs = (P(None, "freq", "src", "rcv"), P(), P(), P(), P(), P("freq"))
    out_specs = (P(None, "freq", "src", "rcv"), P("rcv"))
    return jax.shard_map(functools.partial(body, *sizes), mesh=mesh, in_specs=in_specs, out_specs=out_specs,
                         check_vma=False)
```
